256 devices in a mesh: feat: 8 (over z), dom: 32 (over x, y, core).
Axes of the slice: x: 4, y: 4, z: 8, core: 2. Of those that a mesh axis runs over, the one named last changes fastest.
Arguments:
- features: bfloat16 [128, 32768], P('feat', 'dom'), may hold values from -6 to 6
- self_weight: bfloat16 [128, 512], P('feat'), may hold values from -0.5 to 0.5
- neighbor_weight: bfloat16 [128, 512], P('feat'), may hold values from -0.5 to 0.5
- unit_bias: float32 [512], P('feat'), may hold values from -3 to 3
- send_blocks: int32 [32, 32, 4], P('dom'), may hold values from 0 to 7
- send_counts: int32 [32, 32], P('dom'), may hold values from 0 to 4, as said below
- tile_target: int32 [32, 256], P('dom'), may hold values from 0 to 7
- tile_source: int32 [32, 256], P('dom'), may hold values from 0 to 135, as said below
- tile_count: int32 [32], P('dom'), may hold values from 64 to 256, as said below
- tile_weights: bfloat16 [32, 256, 128, 128], P('dom'), may hold values from 0 to 1, as said below
- out_grad: bfloat16 [512, 32768], P('feat', 'dom'), may hold values from -0.119628906 to 0.119628906
Outputs:
- hidden: bfloat16 [512, 32768], P('feat', 'dom')
- self_gradient: float32 [128, 512], P('feat')
- neighbor_gradient: float32 [128, 512], P('feat')
- bias_gradient: float32 [512], P('feat')
The draws below stay inside these ranges and needn't reach their ends.
Inputs may be any that keep to these rules, and one draw needn't show every extreme that they name: `send_counts`: the diagonal is 0; each partition d fills all 4 slots toward partitions d - 1 and d + 1 (counted round). `tile_count`: at least one partition has all 256 tiles live. `tile_source`: tile 0 of partition d reads slot 8 + ((d + 1) mod 32) * 4, tile 1 reads slot 8 + ((d - 1) mod 32) * 4. `tile_weights`: entries may be 0.
All inputs are finite; a program needn't handle non-finite values.
Results may differ from the reference program's by a relative error of at most 0.005.
Values may be sent and summed in bfloat16 or wider, within the bound.
A program may use at most 64 MiB of HBM per device.

```python
import jax
import jax.numpy as jnp
from jax import lax

F = 128
H = 512
BLK = 128
R = 1024
TILES = 256
BMAX = 4
DOMS = 32
NODES = 32768
RB = 8
NS = 136


def draw_send_counts(key, part):
    key_counts = jax.random.fold_in(key, 21)
    counts = jax.random.randint(key_counts, (DOMS, DOMS), 0, BMAX + 1, dtype=jnp.int32)
    domain_ids = jnp.arange(DOMS, dtype=jnp.int32)
    after = (domain_ids + 1) % DOMS
    before = (domain_ids + DOMS - 1) % DOMS
    near = (domain_ids[None, :] == after[:, None]) | (domain_ids[None, :] == before[:, None])
    counts = jnp.where(near, BMAX, counts)
    counts = jnp.where(domain_ids[:, None] == domain_ids[None, :], 0, counts)
    return counts.astype(jnp.int32)


def draw_tile_source(key, part):
    key_source = jax.random.fold_in(key, 31)
    sources = jax.random.randint(key_source, (DOMS, TILES), 0, NS, dtype=jnp.int32)
    domain_ids = jnp.arange(DOMS, dtype=jnp.int32)
    after_slot = RB + (domain_ids + 1) % DOMS * BMAX
    before_slot = RB + (domain_ids + DOMS - 1) % DOMS * BMAX
    sources = sources.at[:, 0].set(after_slot.astype(jnp.int32))
    sources = sources.at[:, 1].set(before_slot.astype(jnp.int32))
    return sources.astype(jnp.int32)


def draw_tile_count(key, part):
    key_counts = jax.random.fold_in(key, 41)
    key_busiest = jax.random.fold_in(key, 42)
    counts = jax.random.randint(key_counts, (DOMS,), TILES // 4, TILES // 2 + 1, dtype=jnp.int32)
    busiest = jax.random.randint(key_busiest, (), 0, DOMS, dtype=jnp.int32)
    domain_ids = jnp.arange(DOMS, dtype=jnp.int32)
    return jnp.where(domain_ids == busiest, TILES, counts).astype(jnp.int32)


def draw_tile_weights(key, part):
    key_mask = jax.random.fold_in(key, 11)
    key_value = jax.random.fold_in(key, 12)
    shape = (DOMS, TILES, BLK, BLK)
    chance = jax.random.uniform(key_mask, shape, jnp.float32)
    exponent = jax.random.uniform(key_value, shape, jnp.float32, jnp.log(0.03), 0.0)
    values = jnp.exp(exponent)
    kept = chance < 2.0 / BLK
    return jnp.where(kept, values, 0.0).astype(jnp.float32).astype(jnp.bfloat16)


def with_ends(entries, own_key, smallest, high):
    index_at = [jax.random.randint(jax.random.fold_in(own_key, axis), (), 0, length) for axis, length in enumerate(entries.shape)]
    longest = entries.shape.index(max(entries.shape))
    beside = index_at[:longest] + [(index_at[longest] + 1) % entries.shape[longest]] + index_at[longest + 1:]
    return entries.at[tuple(index_at)].set(smallest).at[tuple(beside)].set(high)


def steps_of(key, dims, cuts, least, high):
    factor_of, own = 1.0, jax.random.fold_in(key, 6)
    for axis_at, blocks in cuts:
        heights = jnp.exp(jax.random.uniform(jax.random.fold_in(own, axis_at), (blocks,), jnp.float32, least / len(cuts), high / len(cuts)))
        factor_of = factor_of * jnp.repeat(heights, dims[axis_at] // blocks).reshape([-1 if axis == axis_at else 1 for axis in range(len(dims))])
    return factor_of


def noise(stream_key, dims, width, most, pieces=(), kind=jnp.bfloat16):
    drawn = jax.random.normal(stream_key, dims, jnp.float32) * width
    if len(pieces) > 0:
        drawn = steps_of(stream_key, dims, pieces, -0.22, 0.18) * drawn
    return jnp.clip(drawn, min=-most, max=most).astype(kind)


def setup_inputs(seed: int = 0) -> dict:
    splits = jax.random.split(jax.random.key(seed), 12)
    features = noise(splits[0], (F, NODES), 1.0, 6.0, ((0, 8), (1, 32)))
    self_weight = noise(splits[1], (F, H), F ** -0.5, 0.5, ((0, 8),))
    neighbor_weight = noise(splits[2], (F, H), F ** -0.5, 0.5, ((0, 8),))
    unit_bias = noise(splits[3], (H,), 0.5, 3.0, ((0, 8),), jnp.float32)
    send_blocks = with_ends(jax.random.randint(splits[4], (DOMS, DOMS, BMAX), 0, RB), jax.random.fold_in(splits[4], 1), 0, RB - 1).astype(jnp.int32)
    send_counts = draw_send_counts(jax.random.fold_in(splits[11], 71), 0)
    tile_target = with_ends(jax.random.randint(splits[6], (DOMS, TILES), 0, RB), jax.random.fold_in(splits[6], 1), 0, RB - 1).astype(jnp.int32)
    tile_source = draw_tile_source(jax.random.fold_in(splits[11], 71), 0)
    tile_count = draw_tile_count(jax.random.fold_in(splits[11], 71), 0)
    tile_weights = draw_tile_weights(jax.random.fold_in(splits[11], 71), 0)
    out_grad = noise(splits[10], (H, NODES), 0.02, 0.119628906, ((0, 8), (1, 32)))
    return dict(features=features, self_weight=self_weight, neighbor_weight=neighbor_weight, unit_bias=unit_bias, send_blocks=send_blocks, send_counts=send_counts, tile_target=tile_target, tile_source=tile_source, tile_count=tile_count, tile_weights=tile_weights, out_grad=out_grad)


def activate(values):
    return jax.nn.gelu(values, approximate=True)

def reference(features, self_weight, neighbor_weight, unit_bias, send_blocks, send_counts, tile_target, tile_source, tile_count, tile_weights, out_grad):
    projected = jnp.dot(neighbor_weight.T, features, preferred_element_type=jnp.float32).astype(jnp.bfloat16)
    self_part = jnp.dot(self_weight.T, features, preferred_element_type=jnp.float32)
    unit_blocks = projected.reshape(H, DOMS, RB, BLK)
    slot_index = jnp.arange(BMAX, dtype=jnp.int32)
    domain_ids = jnp.arange(DOMS, dtype=jnp.int32)
    tile_index = jnp.arange(TILES, dtype=jnp.int32)

    def domain(accumulated, domain_index):
        chosen = send_blocks[:, domain_index, :]
        live_slots = slot_index[None, :] < send_counts[:, domain_index][:, None]
        boundary = unit_blocks[:, domain_ids[:, None], chosen, :]
        boundary = jnp.where(live_slots[None, :, :, None], boundary, jnp.zeros((), jnp.bfloat16))
        own_table = unit_blocks[:, domain_index]
        slot_table = jnp.concatenate([own_table, boundary.reshape(H, DOMS * BMAX, BLK)], axis=1)
        weights = tile_weights[domain_index].astype(jnp.float32)
        live_tiles = (tile_index < tile_count[domain_index]).astype(jnp.float32)
        sources = tile_source[domain_index]
        targets = tile_target[domain_index]
        picked = jnp.take(slot_table, sources, axis=1).astype(jnp.float32)
        products = jnp.einsum('htc,trc->thr', picked, weights) * live_tiles[:, None, None]
        aggregate = jax.ops.segment_sum(products, targets, num_segments=RB)
        aggregate = jnp.transpose(aggregate, (1, 0, 2)).reshape(H, R)
        row_sums = lax.optimization_barrier(jnp.sum(weights, axis=2)) * live_tiles[:, None]
        degree = 1.0 + jax.ops.segment_sum(row_sums, targets, num_segments=RB).reshape(R)
        start_col = (domain_index * R).astype(jnp.int32)
        own_self = lax.dynamic_slice_in_dim(self_part, start_col, R, 1)
        summed_input = own_self + aggregate / degree[None, :] + unit_bias[:, None]
        hidden_part, pullback = jax.vjp(activate, summed_input)
        own_grad = lax.dynamic_slice_in_dim(out_grad, start_col, R, 1).astype(jnp.float32)
        summed_grad = pullback(own_grad.astype(summed_input.dtype))[0]
        scaled = (summed_grad / degree[None, :]).astype(jnp.bfloat16)
        target_rows = jnp.take(scaled.reshape(H, RB, BLK), targets, axis=1).astype(jnp.float32)
        pushed = jnp.einsum('htr,trc->thc', target_rows, weights) * live_tiles[:, None, None]
        slot_totals = jax.ops.segment_sum(pushed, sources, num_segments=NS)
        accumulated = accumulated.at[domain_index].add(slot_totals[:RB])
        boundary_totals = slot_totals[RB:].reshape(DOMS, BMAX, H, BLK)
        boundary_totals = boundary_totals * live_slots[:, :, None, None].astype(boundary_totals.dtype)
        accumulated = accumulated.at[domain_ids[:, None], chosen].add(boundary_totals)
        return (accumulated, (hidden_part.astype(jnp.bfloat16), summed_grad))
    initial = jnp.zeros((DOMS, RB, H, BLK), jnp.float32)
    accumulated, (hidden_parts, grad_parts) = lax.scan(domain, initial, domain_ids)
    hidden = jnp.transpose(hidden_parts, (1, 0, 2)).reshape(H, NODES)
    summed_grad = jnp.transpose(grad_parts, (1, 0, 2)).reshape(H, NODES)
    neighbor_totals = jnp.transpose(accumulated, (2, 0, 1, 3)).reshape(H, NODES).astype(jnp.bfloat16)
    narrow_total = summed_grad.astype(jnp.bfloat16)
    self_gradient = jnp.dot(features, narrow_total.T, preferred_element_type=jnp.float32)
    neighbor_gradient = jnp.dot(features, neighbor_totals.T, preferred_element_type=jnp.float32)
    bias_gradient = lax.optimization_barrier(jnp.sum(summed_grad, axis=1))
    return (hidden, self_gradient, neighbor_gradient, bias_gradient)
```

```python
import jax
import jax.numpy as jnp
from jax import lax
from jax.experimental import pallas as pl
from jax.experimental.pallas import tpu as pltpu
from jax.sharding import PartitionSpec as P

BLK = 128
BMAX = 4
NF = 8
ND = 32
RB = 8
NS = 136
TILES = 256
STEP = 8
FR = 16
HU = 64
PIECE = 4
MROWS = RB * FR + FR
BF = jnp.bfloat16
F32 = jnp.float32
MESH = pl.DeviceIdType.MESH
C0 = 0.7978845608028654
C1 = 0.044715


def dot_nt(a, b):
    return lax.dot_general(a, b, (((1,), (1,)), ((), ())), preferred_element_type=F32)


def dot_nn(a, b):
    return lax.dot_general(a, b, (((1,), (0,)), ((), ())), preferred_element_type=F32)


def split3(x):
    hi = x.astype(BF)
    rest = x - hi.astype(F32)
    mid = rest.astype(BF)
    low = (rest - mid.astype(F32)).astype(BF)
    return hi, mid, low


def kernel(
    feat_ref,
    sw_ref,
    nw_ref,
    bias_ref,
    blocks_ref,
    counts_ref,
    target_ref,
    source_ref,
    live_ref,
    tiles_ref,
    grad_ref,
    hidden_ref,
    selfg_ref,
    neighg_ref,
    biasg_ref,
    own,
    sendbuf,
    slots,
    wbuf,
    mask,
    ffull,
    wsend,
    wfull,
    wt,
    abuf,
    afull,
    ubuf,
    gbuf,
    hbuf,
    gsend,
    grecv,
    red,
    fin,
    tile_sem,
    local_sem,
    send_sem,
    recv_sem,
):
    f = lax.axis_index("feat")
    d = lax.axis_index("dom")

    barrier = pltpu.get_barrier_semaphore()

    def greet_dom(i, c):
        e = lax.rem(d + i, ND)
        pl.semaphore_signal(barrier, inc=1, device_id=(f, e), device_id_type=MESH)
        return c

    def greet_feat(i, c):
        g = lax.rem(f + i, NF)
        pl.semaphore_signal(barrier, inc=1, device_id=(g, d), device_id_type=MESH)
        return c

    lax.fori_loop(1, ND, greet_dom, 0)
    lax.fori_loop(1, NF, greet_feat, 0)

    def tile_copy(i):
        part = pl.ds(i * STEP, STEP)
        return pltpu.make_async_copy(tiles_ref.at[0, part], wbuf.at[part], tile_sem.at[i])

    def start_tiles(i, c):
        tile_copy(i).start()
        return c

    lax.fori_loop(0, TILES // STEP, start_tiles, 0)
    grad_copy = pltpu.make_async_copy(grad_ref, gbuf, local_sem.at[0])
    grad_copy.start()

    for b in range(RB):
        block = feat_ref[:, b * BLK : (b + 1) * BLK]
        own[b] = block
        slots[b] = block
        ffull[f, b] = block
    own[RB] = jnp.zeros((FR, BLK), BF)

    def fill(e, c):
        count = counts_ref[0, e]
        for k in range(BMAX):
            pick = jnp.where(k < count, blocks_ref[0, e, k], RB)
            sendbuf[e, k] = own[pick]
        return c

    lax.fori_loop(0, ND, fill, 0)
    slots[pl.ds(RB + BMAX * d, BMAX)] = sendbuf[d]

    for g in range(NF):
        wsend[g] = jnp.concatenate(
            [sw_ref[:, g * HU : (g + 1) * HU], nw_ref[:, g * HU : (g + 1) * HU]], axis=1
        )
    wfull[f] = wsend[f]

    pl.semaphore_wait(barrier, ND - 1 + NF - 1)

    def slot_copy(i):
        e = lax.rem(d + i, ND)
        return pltpu.make_async_remote_copy(
            src_ref=sendbuf.at[e],
            dst_ref=slots.at[pl.ds(RB + BMAX * d, BMAX)],
            send_sem=send_sem.at[0],
            recv_sem=recv_sem.at[0],
            device_id=(f, e),
            device_id_type=MESH,
        )

    def feat_copy(i):
        g = lax.rem(f + i, NF)
        return pltpu.make_async_remote_copy(
            src_ref=own.at[pl.ds(0, RB)],
            dst_ref=ffull.at[f],
            send_sem=send_sem.at[1],
            recv_sem=recv_sem.at[1],
            device_id=(g, d),
            device_id_type=MESH,
        )

    def weight_copy(i):
        g = lax.rem(f + i, NF)
        return pltpu.make_async_remote_copy(
            src_ref=wsend.at[g],
            dst_ref=wfull.at[f],
            send_sem=send_sem.at[2],
            recv_sem=recv_sem.at[2],
            device_id=(g, d),
            device_id_type=MESH,
        )

    def a_copy(i):
        g = lax.rem(f + i, NF)
        return pltpu.make_async_remote_copy(
            src_ref=abuf,
            dst_ref=afull.at[f],
            send_sem=send_sem.at[3],
            recv_sem=recv_sem.at[3],
            device_id=(g, d),
            device_id_type=MESH,
        )

    def part_copy(i):
        e = lax.rem(d + i, ND)
        return pltpu.make_async_remote_copy(
            src_ref=gsend.at[e],
            dst_ref=grecv.at[d],
            send_sem=send_sem.at[4],
            recv_sem=recv_sem.at[4],
            device_id=(f, e),
            device_id_type=MESH,
        )

    plane = d // PIECE
    place = lax.rem(d, PIECE)

    def fin_copy(i):
        e = lax.rem(d + i, ND)
        return pltpu.make_async_remote_copy(
            src_ref=red,
            dst_ref=fin.at[f, place],
            send_sem=send_sem.at[5],
            recv_sem=recv_sem.at[5],
            device_id=(plane, e),
            device_id_type=MESH,
        )

    def start(copy):
        def go(i, c):
            copy(i).start()
            return c

        return go

    def settle(ref, sem):
        pltpu.make_async_copy(ref, ref, sem).wait()

    lax.fori_loop(1, ND, start(slot_copy), 0)
    lax.fori_loop(1, NF, start(weight_copy), 0)
    lax.fori_loop(1, NF, start(feat_copy), 0)

    row = lax.broadcasted_iota(jnp.int32, (MROWS, BLK), 0)
    for j in range(RB):
        inside = ((row >= FR * j) & (row < FR * (j + 1))) | (row == RB * FR + j)
        mask[j] = jnp.where(inside, 1.0, 0.0).astype(BF)
    mask[RB] = jnp.zeros((MROWS, BLK), BF)

    wide = jnp.broadcast_to(bias_ref[...].reshape(1, HU), (BLK, HU))
    wide = jnp.concatenate([wide, jnp.zeros((BLK, BLK - HU), F32)], axis=1)
    bias_cols = jnp.transpose(wide)[:HU]

    settle(slots.at[pl.ds(RB, BMAX * (ND - 1))], recv_sem.at[0])

    live = live_ref[0]
    ones = jnp.ones((FR, BLK), BF)

    def step(i, total):
        tile_copy(i).wait()
        left, right = [], []
        for u in range(STEP):
            t = i * STEP + u
            chosen = slots[source_ref[0, t]]
            where = mask[jnp.where(t < live, target_ref[0, t], RB)]
            left.append(jnp.concatenate([chosen] * RB + [ones], axis=0) * where)
            right.append(wbuf[t])
        return total + dot_nt(jnp.concatenate(left, axis=1), jnp.concatenate(right, axis=1))

    total = lax.fori_loop(0, TILES // STEP, step, jnp.zeros((MROWS, BLK), F32))
    for b in range(RB):
        block = total[b * FR : (b + 1) * FR].astype(BF)
        abuf[b] = block
        afull[f, b] = block
    lax.fori_loop(1, NF, start(a_copy), 0)
    inverse = 1.0 / (1.0 + total[RB * FR : RB * FR + RB])

    settle(wfull.at[pl.ds(0, NF - 1)], recv_sem.at[2])
    settle(ffull.at[pl.ds(0, NF - 1)], recv_sem.at[1])
    wt[...] = jnp.transpose(wfull[...].reshape(NF * FR, BLK).astype(F32)).astype(BF)
    for b in range(RB):
        fb = ffull[:, b].reshape(NF * FR, BLK)
        ubuf[b] = dot_nn(wt[:HU], fb) + bias_cols
    grad_copy.wait()

    settle(afull.at[pl.ds(0, NF - 1)], recv_sem.at[3])

    gtotal = jnp.zeros((NF * FR, BLK), F32)
    btotal = jnp.zeros((HU, BLK), F32)
    nothing = jnp.zeros((HU, BLK), BF)
    for b in range(RB):
        fb = ffull[:, b].reshape(NF * FR, BLK)
        ab = afull[:, b].reshape(NF * FR, BLK)
        inv = inverse[b : b + 1]
        v = ubuf[b] + dot_nn(wt[HU:], ab) * inv
        v2 = v * v
        t = jnp.tanh(C0 * v * (1.0 + C1 * v2))
        half = 0.5 * (1.0 + t)
        hbuf[:, b * BLK : (b + 1) * BLK] = (v * half).astype(BF)
        slope = half + 0.5 * v * (1.0 - t * t) * (C0 * (1.0 + 3.0 * C1 * v2))
        grad = gbuf[:, b * BLK : (b + 1) * BLK].astype(F32) * slope
        btotal = btotal + grad
        narrow = grad.astype(BF)
        scaled = (grad * inv).astype(BF)
        right = jnp.concatenate(
            [
                jnp.concatenate([narrow, nothing], axis=1),
                jnp.concatenate([nothing, scaled], axis=1),
            ],
            axis=0,
        )
        gtotal = gtotal + dot_nt(jnp.concatenate([fb, ab], axis=1), right)
    hidden_copy = pltpu.make_async_copy(hbuf, hidden_ref, local_sem.at[1])
    hidden_copy.start()

    ones8 = jnp.ones((8, BLK), BF)
    brow = jnp.zeros((8, BLK), F32)
    for part in split3(btotal):
        brow = brow + dot_nt(ones8, jnp.concatenate([part, nothing], axis=0))
    for p in range(ND):
        gsend[p, :PIECE] = gtotal[p * PIECE : (p + 1) * PIECE]
        gsend[p, PIECE:] = brow[:PIECE]
    grecv[d] = gsend[d]
    lax.fori_loop(1, ND, start(part_copy), 0)
    settle(grecv.at[pl.ds(0, ND - 1)], recv_sem.at[4])

    added = grecv[0]
    for e in range(1, ND):
        added = added + grecv[e]
    red[...] = added
    biasg_ref[...] = added[PIECE : PIECE + 1, :HU]

    lax.fori_loop(1, ND, start(fin_copy), 0)

    @pl.when(plane != f)
    def _():
        fin_copy(0).start()

    @pl.when(plane == f)
    def _():
        fin[f, place] = red[...]

    @pl.when(plane == f)
    def _():
        settle(grecv.at[pl.ds(0, ND - 1)], recv_sem.at[5])

    @pl.when(plane != f)
    def _():
        settle(grecv, recv_sem.at[5])

    low = lax.broadcasted_iota(jnp.int32, (8, BLK), 0) < PIECE
    near = lax.broadcasted_iota(jnp.int32, (16, BLK), 1) < HU
    rows = []
    for g in range(NF):
        halves = []
        for q in range(0, 4, 2):
            halves.append(jnp.where(low, fin[g, q], pltpu.roll(fin[g, q + 1], 4, 0)))
        rows.append(jnp.concatenate(halves, axis=0))
    for j in range(NF // 2):
        a, b = rows[2 * j], rows[2 * j + 1]
        selfg_ref[:, j * BLK : (j + 1) * BLK] = jnp.where(near, a, pltpu.roll(b, HU, 1))
        neighg_ref[:, j * BLK : (j + 1) * BLK] = jnp.where(near, pltpu.roll(a, HU, 1), b)

    settle(sendbuf.at[pl.ds(0, ND - 1)], send_sem.at[0])
    settle(ffull.at[pl.ds(0, NF - 1)], send_sem.at[1])
    settle(wsend.at[pl.ds(0, NF - 1)], send_sem.at[2])
    settle(afull.at[pl.ds(0, NF - 1)], send_sem.at[3])
    settle(gsend.at[pl.ds(0, ND - 1)], send_sem.at[4])

    @pl.when(plane == f)
    def _():
        settle(gsend.at[pl.ds(0, ND - 1)], send_sem.at[5])

    @pl.when(plane != f)
    def _():
        settle(gsend, send_sem.at[5])

    hidden_copy.wait()


def body(
    features,
    self_weight,
    neighbor_weight,
    unit_bias,
    send_blocks,
    send_counts,
    tile_target,
    tile_source,
    tile_count,
    tile_weights,
    out_grad,
):
    vmem = pl.BlockSpec(memory_space=pltpu.VMEM)
    smem = pl.BlockSpec(memory_space=pltpu.SMEM)
    hbm = pl.BlockSpec(memory_space=pltpu.HBM)
    hidden, selfg, neighg, biasg = pl.pallas_call(
        kernel,
        out_shape=(
            jax.ShapeDtypeStruct((HU, RB * BLK), BF),
            jax.ShapeDtypeStruct((FR, NF * HU), F32),
            jax.ShapeDtypeStruct((FR, NF * HU), F32),
            jax.ShapeDtypeStruct((1, HU), F32),
        ),
        in_specs=[vmem, vmem, vmem, vmem, smem, smem, smem, smem, smem, hbm, hbm],
        out_specs=(hbm, vmem, vmem, vmem),
        scratch_shapes=[
            pltpu.VMEM((RB + 1, FR, BLK), BF),
            pltpu.VMEM((ND, BMAX, FR, BLK), BF),
            pltpu.VMEM((NS, FR, BLK), BF),
            pltpu.VMEM((TILES, BLK, BLK), BF),
            pltpu.VMEM((RB + 1, MROWS, BLK), BF),
            pltpu.VMEM((NF, RB, FR, BLK), BF),
            pltpu.VMEM((NF, FR, BLK), BF),
            pltpu.VMEM((NF, FR, BLK), BF),
            pltpu.VMEM((BLK, NF * FR), BF),
            pltpu.VMEM((RB, FR, BLK), BF),
            pltpu.VMEM((NF, RB, FR, BLK), BF),
            pltpu.VMEM((RB, HU, BLK), F32),
            pltpu.VMEM((HU, RB * BLK), BF),
            pltpu.VMEM((HU, RB * BLK), BF),
            pltpu.VMEM((ND, 8, BLK), F32),
            pltpu.VMEM((ND, 8, BLK), F32),
            pltpu.VMEM((8, BLK), F32),
            pltpu.VMEM((NF, PIECE, 8, BLK), F32),
            pltpu.SemaphoreType.DMA((TILES // STEP,)),
            pltpu.SemaphoreType.DMA((2,)),
            pltpu.SemaphoreType.DMA((6,)),
            pltpu.SemaphoreType.DMA((6,)),
        ],
        compiler_params=pltpu.CompilerParams(
            collective_id=0, has_side_effects=True, vmem_limit_bytes=40 << 20
        ),
    )(
        features,
        self_weight,
        neighbor_weight,
        unit_bias,
        send_blocks,
        send_counts,
        tile_target,
        tile_source,
        tile_count,
        tile_weights,
        out_grad,
    )
    return hidden, selfg, neighg, biasg.reshape(HU)


def solution(mesh):
    in_specs = (
        P("feat", "dom"),
        P("feat", None),
        P("feat", None),
        P("feat"),
        P("dom", None, None),
        P("dom", None),
        P("dom", None),
        P("dom", None),
        P("dom"),
        P("dom", None, None, None),
        P("feat", "dom"),
    )
    out_specs = (P("feat", "dom"), P("feat", None), P("feat", None), P("feat"))
    return jax.shard_map(body, mesh=mesh, in_specs=in_specs, out_specs=out_specs, check_vma=False)
```

```python
import jax
import jax.numpy as jnp
from jax import lax
from jax.experimental import pallas as pl
from jax.experimental.pallas import tpu as pltpu
from jax.sharding import PartitionSpec as P

BLK = 128
BMAX = 4
NF = 8
ND = 32
RB = 8
NS = 136
TILES = 256
STEP = 64
FR = 16
HU = 64
PIECE = 4
MROWS = RB * FR
BF = jnp.bfloat16
F32 = jnp.float32
MESH = pl.DeviceIdType.MESH
C0 = 0.7978845608028654
C1 = 0.044715


def dot_nt(a, b):
    return lax.dot_general(a, b, (((1,), (1,)), ((), ())), preferred_element_type=F32)


def dot_nn(a, b):
    return lax.dot_general(a, b, (((1,), (0,)), ((), ())), preferred_element_type=F32)


def split3(x):
    hi = x.astype(BF)
    rest = x - hi.astype(F32)
    mid = rest.astype(BF)
    low = (rest - mid.astype(F32)).astype(BF)
    return hi, mid, low


def kernel(
    feat_hbm,
    sw_hbm,
    nw_hbm,
    bias_hbm,
    blocks_hbm,
    counts_hbm,
    target_hbm,
    source_hbm,
    live_hbm,
    tiles_ref,
    grad_ref,
    hidden_ref,
    selfg_ref,
    neighg_ref,
    biasg_ref,
    feat_ref,
    sw_ref,
    nw_ref,
    bias_ref,
    blocks_ref,
    counts_ref,
    target_ref,
    source_ref,
    live_ref,
    own,
    sendbuf,
    slots,
    wbuf,
    mask,
    rowmask,
    ffull,
    wsend,
    wfull,
    wt,
    abuf,
    afull,
    ubuf,
    gbuf,
    hbuf,
    gsend,
    grecv,
    red,
    fin,
    selfv,
    neighv,
    biasv,
    tile_sem,
    local_sem,
    send_sem,
    recv_sem,
):
    f = lax.axis_index("feat")
    d = lax.axis_index("dom")

    loads = [
        pltpu.make_async_copy(source, held, local_sem.at[2 + i])
        for i, (source, held) in enumerate(
            [
                (feat_hbm, feat_ref),
                (counts_hbm, counts_ref),
                (blocks_hbm, blocks_ref),
                (sw_hbm, sw_ref),
                (nw_hbm, nw_ref),
                (bias_hbm, bias_ref),
                (target_hbm, target_ref),
                (source_hbm, source_ref),
                (live_hbm, live_ref),
            ]
        )
    ]
    for load in loads:
        load.start()
    barrier = pltpu.get_barrier_semaphore()

    def greet_dom(i, c):
        e = lax.rem(d + i, ND)
        pl.semaphore_signal(barrier, inc=1, device_id=(f, e), device_id_type=MESH)
        return c

    def greet_feat(i, c):
        g = lax.rem(f + i, NF)
        pl.semaphore_signal(barrier, inc=1, device_id=(g, d), device_id_type=MESH)
        return c

    lax.fori_loop(1, ND, greet_dom, 0)
    lax.fori_loop(1, NF, greet_feat, 0)

    def tile_copy(i):
        part = pl.ds(i * STEP, STEP)
        return pltpu.make_async_copy(tiles_ref.at[0, part], wbuf.at[part], tile_sem.at[i])

    def start_tiles(i, c):
        tile_copy(i).start()
        return c

    lax.fori_loop(0, TILES // STEP, start_tiles, 0)
    grad_copy = pltpu.make_async_copy(grad_ref, gbuf, local_sem.at[0])
    grad_copy.start()

    for load in loads:
        load.wait()
    for b in range(RB):
        block = feat_ref[:, b * BLK : (b + 1) * BLK]
        own[b] = block
        slots[b] = block
        ffull[f, b] = block
    own[RB] = jnp.zeros((FR, BLK), BF)

    def fill(e, c):
        count = counts_ref[0, e]
        for k in range(BMAX):
            pick = jnp.where(k < count, blocks_ref[0, k, e], RB)
            sendbuf[e, k] = own[pick]
        return c

    lax.fori_loop(0, ND, fill, 0)
    slots[pl.ds(RB + BMAX * d, BMAX)] = sendbuf[d]

    for g in range(NF):
        wsend[g] = jnp.concatenate(
            [sw_ref[:, g * HU : (g + 1) * HU], nw_ref[:, g * HU : (g + 1) * HU]], axis=1
        )
    wfull[f] = wsend[f]

    pl.semaphore_wait(barrier, ND - 1 + NF - 1)

    def slot_copy(i):
        e = lax.rem(d + i, ND)
        return pltpu.make_async_remote_copy(
            src_ref=sendbuf.at[e],
            dst_ref=slots.at[pl.ds(RB + BMAX * d, BMAX)],
            send_sem=send_sem.at[0],
            recv_sem=recv_sem.at[0],
            device_id=(f, e),
            device_id_type=MESH,
        )

    def feat_copy(i):
        g = lax.rem(f + i, NF)
        return pltpu.make_async_remote_copy(
            src_ref=own.at[pl.ds(0, RB)],
            dst_ref=ffull.at[f],
            send_sem=send_sem.at[1],
            recv_sem=recv_sem.at[1],
            device_id=(g, d),
            device_id_type=MESH,
        )

    def weight_copy(i):
        g = lax.rem(f + i, NF)
        return pltpu.make_async_remote_copy(
            src_ref=wsend.at[g],
            dst_ref=wfull.at[f],
            send_sem=send_sem.at[2],
            recv_sem=recv_sem.at[2],
            device_id=(g, d),
            device_id_type=MESH,
        )

    def a_copy(i):
        g = lax.rem(f + i, NF)
        return pltpu.make_async_remote_copy(
            src_ref=abuf,
            dst_ref=afull.at[f],
            send_sem=send_sem.at[3],
            recv_sem=recv_sem.at[3],
            device_id=(g, d),
            device_id_type=MESH,
        )

    def part_copy(i):
        e = lax.rem(d + i, ND)
        return pltpu.make_async_remote_copy(
            src_ref=gsend.at[e],
            dst_ref=grecv.at[d],
            send_sem=send_sem.at[4],
            recv_sem=recv_sem.at[4],
            device_id=(f, e),
            device_id_type=MESH,
        )

    core = lax.rem(d, 2)
    column = lax.rem(d // 2, 4)
    place = d // 8
    shift = core * (7 - column) + (1 - core) * lax.rem(column + 1, 4)
    plane = lax.rem(f + shift, NF)

    def fin_copy(i):
        e = lax.rem(d + i, ND)
        return pltpu.make_async_remote_copy(
            src_ref=red,
            dst_ref=fin.at[f, place],
            send_sem=send_sem.at[5],
            recv_sem=recv_sem.at[5],
            device_id=(plane, e),
            device_id_type=MESH,
        )

    def start(copy):
        def go(i, c):
            copy(i).start()
            return c

        return go

    def settle(ref, sem):
        pltpu.make_async_copy(ref, ref, sem).wait()

    lax.fori_loop(1, ND, start(slot_copy), 0)
    lax.fori_loop(1, NF, start(weight_copy), 0)
    lax.fori_loop(1, NF, start(feat_copy), 0)

    row = lax.broadcasted_iota(jnp.int32, (MROWS, BLK), 0)
    top = lax.broadcasted_iota(jnp.int32, (FR, BLK), 0)
    for j in range(RB):
        mask[j] = jnp.where((row >= FR * j) & (row < FR * (j + 1)), 1.0, 0.0).astype(BF)
        rowmask[j] = jnp.where(top == j, 1.0, 0.0).astype(BF)
    mask[RB] = jnp.zeros((MROWS, BLK), BF)
    rowmask[RB] = jnp.zeros((FR, BLK), BF)
    live = live_ref[0, 0]

    def goal(t):
        return jnp.where(t < live, target_ref[0, t], RB)

    def degree_step(i, total):
        tile_copy(i).wait()
        left = [rowmask[goal(i * STEP + u)] for u in range(STEP)]
        right = [wbuf[i * STEP + u] for u in range(STEP)]
        return total + dot_nt(jnp.concatenate(left, axis=1), jnp.concatenate(right, axis=1))

    degrees = lax.fori_loop(0, TILES // STEP, degree_step, jnp.zeros((FR, BLK), F32))
    inverse = 1.0 / (1.0 + degrees)

    wide = jnp.broadcast_to(bias_ref[...].reshape(1, HU), (BLK, HU))
    wide = jnp.concatenate([wide, jnp.zeros((BLK, BLK - HU), F32)], axis=1)
    bias_cols = jnp.transpose(wide)[:HU]

    settle(slots.at[pl.ds(RB, BMAX * (ND - 1))], recv_sem.at[0])

    def step(i, total):
        left, right = [], []
        for u in range(STEP):
            t = i * STEP + u
            chosen = slots[source_ref[0, t]]
            left.append(jnp.concatenate([chosen] * RB, axis=0) * mask[goal(t)])
            right.append(wbuf[t])
        return total + dot_nt(jnp.concatenate(left, axis=1), jnp.concatenate(right, axis=1))

    total = lax.fori_loop(0, TILES // STEP, step, jnp.zeros((MROWS, BLK), F32))
    for b in range(RB):
        block = total[b * FR : (b + 1) * FR].astype(BF)
        abuf[b] = block
        afull[f, b] = block
    lax.fori_loop(1, NF, start(a_copy), 0)

    settle(wfull.at[pl.ds(0, NF - 1)], recv_sem.at[2])
    settle(ffull.at[pl.ds(0, NF - 1)], recv_sem.at[1])
    wt[...] = jnp.transpose(wfull[...].reshape(NF * FR, BLK).astype(F32)).astype(BF)
    for b in range(RB):
        fb = ffull[:, b].reshape(NF * FR, BLK)
        ubuf[b] = dot_nn(wt[:HU], fb) + bias_cols
    grad_copy.wait()

    settle(afull.at[pl.ds(0, NF - 1)], recv_sem.at[3])

    gtotal = jnp.zeros((NF * FR, BLK), F32)
    btotal = jnp.zeros((HU, BLK), F32)
    nothing = jnp.zeros((HU, BLK), BF)
    for b in range(RB):
        fb = ffull[:, b].reshape(NF * FR, BLK)
        ab = afull[:, b].reshape(NF * FR, BLK)
        inv = inverse[b : b + 1]
        v = ubuf[b] + dot_nn(wt[HU:], ab) * inv
        v2 = v * v
        t = jnp.tanh(C0 * v * (1.0 + C1 * v2))
        half = 0.5 * (1.0 + t)
        hbuf[:, b * BLK : (b + 1) * BLK] = (v * half).astype(BF)
        slope = half + 0.5 * v * (1.0 - t * t) * (C0 * (1.0 + 3.0 * C1 * v2))
        grad = gbuf[:, b * BLK : (b + 1) * BLK].astype(F32) * slope
        btotal = btotal + grad
        narrow = grad.astype(BF)
        scaled = (grad * inv).astype(BF)
        right = jnp.concatenate(
            [
                jnp.concatenate([narrow, nothing], axis=1),
                jnp.concatenate([nothing, scaled], axis=1),
            ],
            axis=0,
        )
        gtotal = gtotal + dot_nt(jnp.concatenate([fb, ab], axis=1), right)
    hidden_copy = pltpu.make_async_copy(hbuf, hidden_ref, local_sem.at[1])
    hidden_copy.start()

    ones8 = jnp.ones((8, BLK), BF)
    brow = jnp.zeros((8, BLK), F32)
    for part in split3(btotal):
        brow = brow + dot_nt(ones8, jnp.concatenate([part, nothing], axis=0))
    for g in range(NF):
        away = lax.rem(g - f + NF, NF)
        odd = away // 4
        near = odd * (7 - away) + (1 - odd) * lax.rem(away + 3, 4)
        for q in range(PIECE):
            p = (q * 4 + near) * 2 + odd
            gsend[p, :PIECE] = gtotal[g * FR + q * PIECE : g * FR + (q + 1) * PIECE]
            gsend[p, PIECE:] = brow[:PIECE]
    grecv[d] = gsend[d]
    lax.fori_loop(1, ND, start(part_copy), 0)
    settle(grecv.at[pl.ds(0, ND - 1)], recv_sem.at[4])

    added = grecv[0]
    for e in range(1, ND):
        added = added + grecv[e]
    red[...] = added[:PIECE]
    biasv[...] = added[PIECE : PIECE + 1, :HU]
    bias_copy = pltpu.make_async_copy(biasv, biasg_ref, local_sem.at[11])
    bias_copy.start()

    lax.fori_loop(1, ND, start(fin_copy), 0)

    @pl.when(shift != 0)
    def _():
        fin_copy(0).start()

    @pl.when(shift == 0)
    def _():
        fin[f, place] = red[...]

    flat = fin.reshape(ND, PIECE, BLK)

    @pl.when(shift == 0)
    def _():
        settle(flat.at[pl.ds(0, ND - 1)], recv_sem.at[5])

    @pl.when(shift != 0)
    def _():
        settle(flat, recv_sem.at[5])

    rows = [jnp.concatenate([fin[g, q] for q in range(PIECE)], axis=0) for g in range(NF)]
    for j in range(0, NF, 2):
        a, b = rows[j], rows[j + 1]
        at = slice(j * HU, (j + 2) * HU)
        selfv[:, at] = jnp.concatenate([a[:, :HU], b[:, :HU]], axis=1)
        neighv[:, at] = jnp.concatenate([a[:, HU:], b[:, HU:]], axis=1)
    self_copy = pltpu.make_async_copy(selfv, selfg_ref, local_sem.at[12])
    self_copy.start()
    neigh_copy = pltpu.make_async_copy(neighv, neighg_ref, local_sem.at[13])
    neigh_copy.start()

    settle(sendbuf.at[pl.ds(0, ND - 1)], send_sem.at[0])
    settle(ffull.at[pl.ds(0, NF - 1)], send_sem.at[1])
    settle(wsend.at[pl.ds(0, NF - 1)], send_sem.at[2])
    settle(afull.at[pl.ds(0, NF - 1)], send_sem.at[3])
    settle(gsend.at[pl.ds(0, ND - 1)], send_sem.at[4])


    @pl.when(shift == 0)
    def _():
        settle(flat.at[pl.ds(0, ND - 1)], send_sem.at[5])

    @pl.when(shift != 0)
    def _():
        settle(flat, send_sem.at[5])

    for copy in (bias_copy, hidden_copy, self_copy, neigh_copy):
        copy.wait()


def hand_over(*refs):
    sems = refs[-1]
    copies = [pltpu.make_async_copy(refs[i], refs[4 + i], sems.at[i]) for i in range(4)]
    for copy in copies:
        copy.start()
    for copy in copies:
        copy.wait()


def body(
    features,
    self_weight,
    neighbor_weight,
    unit_bias,
    send_blocks,
    send_counts,
    tile_target,
    tile_source,
    tile_count,
    tile_weights,
    out_grad,
):
    hbm = pl.BlockSpec(memory_space=pltpu.HBM)
    shapes = (
        jax.ShapeDtypeStruct((HU, RB * BLK), BF),
        jax.ShapeDtypeStruct((FR, NF * HU), F32),
        jax.ShapeDtypeStruct((FR, NF * HU), F32),
        jax.ShapeDtypeStruct((1, HU), F32),
    )
    made = pl.pallas_call(
        kernel,
        out_shape=shapes,
        in_specs=[hbm] * 11,
        out_specs=(hbm,) * 4,
        scratch_shapes=[
            pltpu.VMEM((FR, RB * BLK), BF),
            pltpu.VMEM((FR, NF * HU), BF),
            pltpu.VMEM((FR, NF * HU), BF),
            pltpu.VMEM((HU,), F32),
            pltpu.SMEM((1, BMAX, ND), jnp.int32),
            pltpu.SMEM((1, ND), jnp.int32),
            pltpu.SMEM((1, TILES), jnp.int32),
            pltpu.SMEM((1, TILES), jnp.int32),
            pltpu.SMEM((1, 1), jnp.int32),
            pltpu.VMEM((RB + 1, FR, BLK), BF),
            pltpu.VMEM((ND, BMAX, FR, BLK), BF),
            pltpu.VMEM((NS, FR, BLK), BF),
            pltpu.VMEM((TILES, BLK, BLK), BF),
            pltpu.VMEM((RB + 1, MROWS, BLK), BF),
            pltpu.VMEM((RB + 1, FR, BLK), BF),
            pltpu.VMEM((NF, RB, FR, BLK), BF),
            pltpu.VMEM((NF, FR, BLK), BF),
            pltpu.VMEM((NF, FR, BLK), BF),
            pltpu.VMEM((BLK, NF * FR), BF),
            pltpu.VMEM((RB, FR, BLK), BF),
            pltpu.VMEM((NF, RB, FR, BLK), BF),
            pltpu.VMEM((RB, HU, BLK), F32),
            pltpu.VMEM((HU, RB * BLK), BF),
            pltpu.VMEM((HU, RB * BLK), BF),
            pltpu.VMEM((ND, 8, BLK), F32),
            pltpu.VMEM((ND, 8, BLK), F32),
            pltpu.VMEM((PIECE, BLK), F32),
            pltpu.VMEM((NF, PIECE, PIECE, BLK), F32),
            pltpu.VMEM((FR, NF * HU), F32),
            pltpu.VMEM((FR, NF * HU), F32),
            pltpu.VMEM((1, HU), F32),
            pltpu.SemaphoreType.DMA((TILES // STEP,)),
            pltpu.SemaphoreType.DMA((14,)),
            pltpu.SemaphoreType.DMA((6,)),
            pltpu.SemaphoreType.DMA((6,)),
        ],
        compiler_params=pltpu.CompilerParams(
            collective_id=0, has_side_effects=True, vmem_limit_bytes=60 << 20
        ),
    )(
        features,
        self_weight,
        neighbor_weight,
        unit_bias,
        jnp.transpose(send_blocks, (0, 2, 1)),
        send_counts,
        tile_target,
        tile_source,
        tile_count.reshape(1, 1),
        tile_weights,
        out_grad,
    )
    hidden, selfg, neighg, biasg = pl.pallas_call(
        hand_over,
        out_shape=shapes,
        in_specs=[hbm] * 4,
        out_specs=(hbm,) * 4,
        scratch_shapes=[pltpu.SemaphoreType.DMA((4,))],
    )(*made)
    return hidden, selfg, neighg, biasg.reshape(HU)


def solution(mesh):
    in_specs = (
        P("feat", "dom"),
        P("feat", None),
        P("feat", None),
        P("feat"),
        P("dom", None, None),
        P("dom", None),
        P("dom", None),
        P("dom", None),
        P("dom"),
        P("dom", None, None, None),
        P("feat", "dom"),
    )
    out_specs = (P("feat", "dom"), P("feat", None), P("feat", None), P("feat"))
    return jax.shard_map(body, mesh=mesh, in_specs=in_specs, out_specs=out_specs, check_vma=False)
```

```python
import jax
import jax.numpy as jnp
from jax import lax
from jax.experimental import pallas as pl
from jax.experimental.pallas import tpu as pltpu
from jax.sharding import PartitionSpec as P

BLK = 128
BMAX = 4
NF = 8
ND = 32
RB = 8
NS = 136
TILES = 256
STEP = 64
FR = 16
HU = 64
PIECE = 4
MROWS = RB * FR
BF = jnp.bfloat16
F32 = jnp.float32
MESH = pl.DeviceIdType.MESH
C0 = 0.7978845608028654
C1 = 0.044715


def dot_nt(a, b):
    return lax.dot_general(a, b, (((1,), (1,)), ((), ())), preferred_element_type=F32)


def dot_nn(a, b):
    return lax.dot_general(a, b, (((1,), (0,)), ((), ())), preferred_element_type=F32)


def split3(x):
    hi = x.astype(BF)
    rest = x - hi.astype(F32)
    mid = rest.astype(BF)
    low = (rest - mid.astype(F32)).astype(BF)
    return hi, mid, low


def kernel(
    feat_hbm,
    sw_hbm,
    nw_hbm,
    bias_hbm,
    blocks_hbm,
    counts_hbm,
    target_hbm,
    source_hbm,
    live_hbm,
    tiles_ref,
    grad_ref,
    hidden_ref,
    selfg_ref,
    neighg_ref,
    biasg_ref,
    feat_ref,
    sw_ref,
    nw_ref,
    bias_ref,
    blocks_ref,
    counts_ref,
    target_ref,
    source_ref,
    live_ref,
    own,
    sendbuf,
    slots,
    wbuf,
    mask,
    rowmask,
    ffull,
    wsend,
    wfull,
    wt,
    abuf,
    afull,
    ubuf,
    gbuf,
    hbuf,
    gsend,
    grecv,
    red,
    fin,
    selfv,
    neighv,
    biasv,
    tile_sem,
    local_sem,
    send_sem,
    recv_sem,
):
    f = lax.axis_index("feat")
    d = lax.axis_index("dom")

    loads = [
        pltpu.make_async_copy(source, held, local_sem.at[2 + i])
        for i, (source, held) in enumerate(
            [
                (feat_hbm, feat_ref),
                (counts_hbm, counts_ref),
                (blocks_hbm, blocks_ref),
                (sw_hbm, sw_ref),
                (nw_hbm, nw_ref),
                (bias_hbm, bias_ref),
                (target_hbm, target_ref),
                (source_hbm, source_ref),
                (live_hbm, live_ref),
            ]
        )
    ]
    for load in loads:
        load.start()
    barrier = pltpu.get_barrier_semaphore()

    def greet_dom(i, c):
        e = lax.rem(d + i, ND)
        pl.semaphore_signal(barrier, inc=1, device_id=(f, e), device_id_type=MESH)
        return c

    def greet_feat(i, c):
        g = lax.rem(f + i, NF)
        pl.semaphore_signal(barrier, inc=1, device_id=(g, d), device_id_type=MESH)
        return c

    lax.fori_loop(1, ND, greet_dom, 0)
    lax.fori_loop(1, NF, greet_feat, 0)

    def tile_copy(i):
        part = pl.ds(i * STEP, STEP)
        return pltpu.make_async_copy(tiles_ref.at[0, part], wbuf.at[part], tile_sem.at[i])

    def start_tiles(i, c):
        tile_copy(i).start()
        return c

    lax.fori_loop(0, TILES // STEP, start_tiles, 0)
    grad_copy = pltpu.make_async_copy(grad_ref, gbuf, local_sem.at[0])
    grad_copy.start()

    for load in loads:
        load.wait()
    for b in range(RB):
        block = feat_ref[:, b * BLK : (b + 1) * BLK]
        own[b] = block
        slots[b] = block
        ffull[f, b] = block
    own[RB] = jnp.zeros((FR, BLK), BF)

    def fill(e, c):
        count = counts_ref[0, e]
        for k in range(BMAX):
            pick = jnp.where(k < count, blocks_ref[0, k, e], RB)
            sendbuf[e, k] = own[pick]
        return c

    lax.fori_loop(0, ND, fill, 0)
    slots[pl.ds(RB + BMAX * d, BMAX)] = sendbuf[d]

    for g in range(NF):
        wsend[g] = jnp.concatenate(
            [sw_ref[:, g * HU : (g + 1) * HU], nw_ref[:, g * HU : (g + 1) * HU]], axis=1
        )
    wfull[f] = wsend[f]

    pl.semaphore_wait(barrier, ND - 1 + NF - 1)

    def slot_copy(i):
        e = lax.rem(d + i, ND)
        return pltpu.make_async_remote_copy(
            src_ref=sendbuf.at[e],
            dst_ref=slots.at[pl.ds(RB + BMAX * d, BMAX)],
            send_sem=send_sem.at[0],
            recv_sem=recv_sem.at[0],
            device_id=(f, e),
            device_id_type=MESH,
        )

    def feat_copy(i):
        g = lax.rem(f + i, NF)
        return pltpu.make_async_remote_copy(
            src_ref=own.at[pl.ds(0, RB)],
            dst_ref=ffull.at[f],
            send_sem=send_sem.at[1],
            recv_sem=recv_sem.at[1],
            device_id=(g, d),
            device_id_type=MESH,
        )

    def weight_copy(i):
        g = lax.rem(f + i, NF)
        return pltpu.make_async_remote_copy(
            src_ref=wsend.at[g],
            dst_ref=wfull.at[f],
            send_sem=send_sem.at[2],
            recv_sem=recv_sem.at[2],
            device_id=(g, d),
            device_id_type=MESH,
        )

    def a_copy(i):
        g = lax.rem(f + i, NF)
        return pltpu.make_async_remote_copy(
            src_ref=abuf,
            dst_ref=afull.at[f],
            send_sem=send_sem.at[3],
            recv_sem=recv_sem.at[3],
            device_id=(g, d),
            device_id_type=MESH,
        )

    def part_copy(i):
        e = lax.rem(d + i, ND)
        return pltpu.make_async_remote_copy(
            src_ref=gsend.at[e],
            dst_ref=grecv.at[d],
            send_sem=send_sem.at[4],
            recv_sem=recv_sem.at[4],
            device_id=(f, e),
            device_id_type=MESH,
        )

    core = lax.rem(d, 2)
    column = lax.rem(d // 2, 4)
    place = d // 8
    shift = core * (7 - column) + (1 - core) * lax.rem(column + 1, 4)
    plane = lax.rem(f + shift, NF)

    def fin_copy(i):
        e = lax.rem(d + i, ND)
        return pltpu.make_async_remote_copy(
            src_ref=red,
            dst_ref=fin.at[f, place],
            send_sem=send_sem.at[5],
            recv_sem=recv_sem.at[5],
            device_id=(plane, e),
            device_id_type=MESH,
        )

    def start(copy):
        def go(i, c):
            copy(i).start()
            return c

        return go

    def settle(ref, sem):
        pltpu.make_async_copy(ref, ref, sem).wait()

    lax.fori_loop(1, ND, start(slot_copy), 0)
    lax.fori_loop(1, NF, start(weight_copy), 0)
    lax.fori_loop(1, NF, start(feat_copy), 0)

    row = lax.broadcasted_iota(jnp.int32, (MROWS, BLK), 0)
    top = lax.broadcasted_iota(jnp.int32, (FR, BLK), 0)
    for j in range(RB):
        mask[j] = jnp.where((row >= FR * j) & (row < FR * (j + 1)), 1.0, 0.0).astype(BF)
        rowmask[j] = jnp.where(top == j, 1.0, 0.0).astype(BF)
    mask[RB] = jnp.zeros((MROWS, BLK), BF)
    rowmask[RB] = jnp.zeros((FR, BLK), BF)
    live = live_ref[0, 0]

    def goal(t):
        return jnp.where(t < live, target_ref[0, t], RB)

    def degree_step(i, total):
        tile_copy(i).wait()
        left = [rowmask[goal(i * STEP + u)] for u in range(STEP)]
        right = [wbuf[i * STEP + u] for u in range(STEP)]
        return total + dot_nt(jnp.concatenate(left, axis=1), jnp.concatenate(right, axis=1))

    degrees = lax.fori_loop(0, TILES // STEP, degree_step, jnp.zeros((FR, BLK), F32))
    inverse = 1.0 / (1.0 + degrees)

    wide = jnp.broadcast_to(bias_ref[...].reshape(1, HU), (BLK, HU))
    wide = jnp.concatenate([wide, jnp.zeros((BLK, BLK - HU), F32)], axis=1)
    bias_cols = jnp.transpose(wide)[:HU]

    settle(slots.at[pl.ds(RB, BMAX * (ND - 1))], recv_sem.at[0])

    def step(i, total):
        left, right = [], []
        for u in range(STEP):
            t = i * STEP + u
            chosen = slots[source_ref[0, t]]
            left.append(jnp.concatenate([chosen] * RB, axis=0) * mask[goal(t)])
            right.append(wbuf[t])
        return total + dot_nt(jnp.concatenate(left, axis=1), jnp.concatenate(right, axis=1))

    total = lax.fori_loop(0, TILES // STEP, step, jnp.zeros((MROWS, BLK), F32))
    for b in range(RB):
        block = total[b * FR : (b + 1) * FR].astype(BF)
        abuf[b] = block
        afull[f, b] = block
    lax.fori_loop(1, NF, start(a_copy), 0)

    settle(wfull.at[pl.ds(0, NF - 1)], recv_sem.at[2])
    settle(ffull.at[pl.ds(0, NF - 1)], recv_sem.at[1])
    wt[...] = jnp.transpose(wfull[...].reshape(NF * FR, BLK).astype(F32)).astype(BF)
    for b in range(RB):
        fb = ffull[:, b].reshape(NF * FR, BLK)
        ubuf[b] = dot_nn(wt[:HU], fb) + bias_cols
    grad_copy.wait()

    settle(afull.at[pl.ds(0, NF - 1)], recv_sem.at[3])

    gtotal = jnp.zeros((NF * FR, BLK), F32)
    btotal = jnp.zeros((HU, BLK), F32)
    nothing = jnp.zeros((HU, BLK), BF)
    for b in range(RB):
        fb = ffull[:, b].reshape(NF * FR, BLK)
        ab = afull[:, b].reshape(NF * FR, BLK)
        inv = inverse[b : b + 1]
        v = ubuf[b] + dot_nn(wt[HU:], ab) * inv
        v2 = v * v
        t = jnp.tanh(C0 * v * (1.0 + C1 * v2))
        half = 0.5 * (1.0 + t)
        hbuf[:, b * BLK : (b + 1) * BLK] = (v * half).astype(BF)
        slope = half + 0.5 * v * (1.0 - t * t) * (C0 * (1.0 + 3.0 * C1 * v2))
        grad = gbuf[:, b * BLK : (b + 1) * BLK].astype(F32) * slope
        btotal = btotal + grad
        narrow = grad.astype(BF)
        scaled = (grad * inv).astype(BF)
        right = jnp.concatenate(
            [
                jnp.concatenate([narrow, nothing], axis=1),
                jnp.concatenate([nothing, scaled], axis=1),
            ],
            axis=0,
        )
        gtotal = gtotal + dot_nt(jnp.concatenate([fb, ab], axis=1), right)
    hidden_copy = pltpu.make_async_copy(hbuf, hidden_ref, local_sem.at[1])
    hidden_copy.start()

    ones8 = jnp.ones((8, BLK), BF)
    brow = jnp.zeros((8, BLK), F32)
    for part in split3(btotal):
        brow = brow + dot_nt(ones8, jnp.concatenate([part, nothing], axis=0))
    for g in range(NF):
        away = lax.rem(g - f + NF, NF)
        odd = away // 4
        near = odd * (7 - away) + (1 - odd) * lax.rem(away + 3, 4)
        for q in range(PIECE):
            p = (q * 4 + near) * 2 + odd
            gsend[p, :PIECE] = gtotal[g * FR + q * PIECE : g * FR + (q + 1) * PIECE]
            gsend[p, PIECE:] = brow[:PIECE]
    grecv[d] = gsend[d]
    lax.fori_loop(1, ND, start(part_copy), 0)
    settle(grecv.at[pl.ds(0, ND - 1)], recv_sem.at[4])

    added = grecv[0]
    for e in range(1, ND):
        added = added + grecv[e]
    red[...] = added[:PIECE]
    biasv[...] = added[PIECE : PIECE + 1, :HU]
    bias_copy = pltpu.make_async_copy(biasv, biasg_ref, local_sem.at[11])
    bias_copy.start()

    lax.fori_loop(1, ND, start(fin_copy), 0)

    @pl.when(shift != 0)
    def _():
        fin_copy(0).start()

    @pl.when(shift == 0)
    def _():
        fin[f, place] = red[...]

    flat = fin.reshape(ND, PIECE, BLK)

    @pl.when(shift == 0)
    def _():
        settle(flat.at[pl.ds(0, ND - 1)], recv_sem.at[5])

    @pl.when(shift != 0)
    def _():
        settle(flat, recv_sem.at[5])

    rows = [jnp.concatenate([fin[g, q] for q in range(PIECE)], axis=0) for g in range(NF)]
    for j in range(0, NF, 2):
        a, b = rows[j], rows[j + 1]
        at = slice(j * HU, (j + 2) * HU)
        selfv[:, at] = jnp.concatenate([a[:, :HU], b[:, :HU]], axis=1)
        neighv[:, at] = jnp.concatenate([a[:, HU:], b[:, HU:]], axis=1)
    self_copy = pltpu.make_async_copy(selfv, selfg_ref, local_sem.at[12])
    self_copy.start()
    neigh_copy = pltpu.make_async_copy(neighv, neighg_ref, local_sem.at[13])
    neigh_copy.start()

    settle(sendbuf.at[pl.ds(0, ND - 1)], send_sem.at[0])
    settle(ffull.at[pl.ds(0, NF - 1)], send_sem.at[1])
    settle(wsend.at[pl.ds(0, NF - 1)], send_sem.at[2])
    settle(afull.at[pl.ds(0, NF - 1)], send_sem.at[3])
    settle(gsend.at[pl.ds(0, ND - 1)], send_sem.at[4])


    @pl.when(shift == 0)
    def _():
        settle(flat.at[pl.ds(0, ND - 1)], send_sem.at[5])

    @pl.when(shift != 0)
    def _():
        settle(flat, send_sem.at[5])

    for copy in (bias_copy, hidden_copy, self_copy, neigh_copy):
        copy.wait()


def hand_over(*refs):
    for made, out in zip(refs[:4], refs[4:]):
        out[...] = made[...]


def body(
    features,
    self_weight,
    neighbor_weight,
    unit_bias,
    send_blocks,
    send_counts,
    tile_target,
    tile_source,
    tile_count,
    tile_weights,
    out_grad,
):
    hbm = pl.BlockSpec(memory_space=pltpu.HBM)
    vmem = pl.BlockSpec(memory_space=pltpu.VMEM)
    shapes = (
        jax.ShapeDtypeStruct((HU, RB * BLK), BF),
        jax.ShapeDtypeStruct((FR, NF * HU), F32),
        jax.ShapeDtypeStruct((FR, NF * HU), F32),
        jax.ShapeDtypeStruct((1, HU), F32),
    )
    made = pl.pallas_call(
        kernel,
        out_shape=tuple(pltpu.VMEM(one.shape, one.dtype) for one in shapes),
        in_specs=[hbm] * 11,
        out_specs=(vmem,) * 4,
        scratch_shapes=[
            pltpu.VMEM((FR, RB * BLK), BF),
            pltpu.VMEM((FR, NF * HU), BF),
            pltpu.VMEM((FR, NF * HU), BF),
            pltpu.VMEM((HU,), F32),
            pltpu.SMEM((1, BMAX, ND), jnp.int32),
            pltpu.SMEM((1, ND), jnp.int32),
            pltpu.SMEM((1, TILES), jnp.int32),
            pltpu.SMEM((1, TILES), jnp.int32),
            pltpu.SMEM((1, 1), jnp.int32),
            pltpu.VMEM((RB + 1, FR, BLK), BF),
            pltpu.VMEM((ND, BMAX, FR, BLK), BF),
            pltpu.VMEM((NS, FR, BLK), BF),
            pltpu.VMEM((TILES, BLK, BLK), BF),
            pltpu.VMEM((RB + 1, MROWS, BLK), BF),
            pltpu.VMEM((RB + 1, FR, BLK), BF),
            pltpu.VMEM((NF, RB, FR, BLK), BF),
            pltpu.VMEM((NF, FR, BLK), BF),
            pltpu.VMEM((NF, FR, BLK), BF),
            pltpu.VMEM((BLK, NF * FR), BF),
            pltpu.VMEM((RB, FR, BLK), BF),
            pltpu.VMEM((NF, RB, FR, BLK), BF),
            pltpu.VMEM((RB, HU, BLK), F32),
            pltpu.VMEM((HU, RB * BLK), BF),
            pltpu.VMEM((HU, RB * BLK), BF),
            pltpu.VMEM((ND, 8, BLK), F32),
            pltpu.VMEM((ND, 8, BLK), F32),
            pltpu.VMEM((PIECE, BLK), F32),
            pltpu.VMEM((NF, PIECE, PIECE, BLK), F32),
            pltpu.VMEM((FR, NF * HU), F32),
            pltpu.VMEM((FR, NF * HU), F32),
            pltpu.VMEM((1, HU), F32),
            pltpu.SemaphoreType.DMA((TILES // STEP,)),
            pltpu.SemaphoreType.DMA((14,)),
            pltpu.SemaphoreType.DMA((6,)),
            pltpu.SemaphoreType.DMA((6,)),
        ],
        compiler_params=pltpu.CompilerParams(
            collective_id=0, has_side_effects=True, vmem_limit_bytes=60 << 20
        ),
    )(
        features,
        self_weight,
        neighbor_weight,
        unit_bias,
        jnp.transpose(send_blocks, (0, 2, 1)),
        send_counts,
        tile_target,
        tile_source,
        tile_count.reshape(1, 1),
        tile_weights,
        out_grad,
    )
    hidden, selfg, neighg, biasg = pl.pallas_call(
        hand_over,
        out_shape=shapes,
        in_specs=[vmem] * 4,
        out_specs=(vmem,) * 4,
    )(*[pltpu.with_memory_space_constraint(one, pltpu.VMEM) for one in made])
    return hidden, selfg, neighg, biasg.reshape(HU)


def solution(mesh):
    in_specs = (
        P("feat", "dom"),
        P("feat", None),
        P("feat", None),
        P("feat"),
        P("dom", None, None),
        P("dom", None),
        P("dom", None),
        P("dom", None),
        P("dom"),
        P("dom", None, None, None),
        P("feat", "dom"),
    )
    out_specs = (P("feat", "dom"), P("feat", None), P("feat", None), P("feat"))
    return jax.shard_map(body, mesh=mesh, in_specs=in_specs, out_specs=out_specs, check_vma=False)
```

```python
import jax
import jax.numpy as jnp
from jax import lax
from jax.experimental import pallas as pl
from jax.experimental.pallas import tpu as pltpu
from jax.sharding import PartitionSpec as P

BLK = 128
BMAX = 4
NF = 8
ND = 32
RB = 8
NS = 136
TILES = 256
STEP = 64
FR = 16
HU = 64
PIECE = 4
HALF = FR // 2
MROWS = RB * HALF


def around(n, i):
    return min(i, n - i)


PLANE = sorted(
    ((x, y, c) for x in range(4) for y in range(4) for c in range(2)),
    key=lambda p: (-around(4, p[0]) - around(4, p[1]), -p[2]),
)
OTHERS = [p for p in PLANE if any(p)]
COLUMN = sorted(range(1, NF), key=lambda z: -around(NF, z))
BF = jnp.bfloat16
F32 = jnp.float32
MESH = pl.DeviceIdType.MESH
C0 = 0.7978845608028654
C1 = 0.044715


def dot_nt(a, b):
    return lax.dot_general(a, b, (((1,), (1,)), ((), ())), preferred_element_type=F32)


def dot_nn(a, b):
    return lax.dot_general(a, b, (((1,), (0,)), ((), ())), preferred_element_type=F32)


def split3(x):
    hi = x.astype(BF)
    rest = x - hi.astype(F32)
    mid = rest.astype(BF)
    low = (rest - mid.astype(F32)).astype(BF)
    return hi, mid, low


def kernel(
    feat_hbm,
    sw_hbm,
    nw_hbm,
    bias_hbm,
    blocks_hbm,
    counts_hbm,
    target_hbm,
    source_hbm,
    live_hbm,
    tiles_ref,
    grad_ref,
    hidden_ref,
    selfg_ref,
    neighg_ref,
    biasg_ref,
    feat_ref,
    sw_ref,
    nw_ref,
    bias_ref,
    blocks_ref,
    counts_ref,
    target_ref,
    source_ref,
    live_ref,
    own,
    sendbuf,
    slots,
    twice,
    wbuf,
    mask,
    rowmask,
    ffull,
    wsend,
    wfull,
    wt,
    abuf,
    afull,
    ubuf,
    gbuf,
    hbuf,
    gsend,
    grecv,
    red,
    fin,
    selfv,
    neighv,
    biasv,
    tile_sem,
    local_sem,
    send_sem,
    recv_sem,
):
    f = lax.axis_index("feat")
    d = lax.axis_index("dom")

    loads = [
        pltpu.make_async_copy(source, held, local_sem.at[2 + i])
        for i, (source, held) in enumerate(
            [
                (feat_hbm, feat_ref),
                (counts_hbm, counts_ref),
                (blocks_hbm, blocks_ref),
                (sw_hbm, sw_ref),
                (nw_hbm, nw_ref),
                (bias_hbm, bias_ref),
                (target_hbm, target_ref),
                (source_hbm, source_ref),
                (live_hbm, live_ref),
            ]
        )
    ]
    for load in loads:
        load.start()
    barrier = pltpu.get_barrier_semaphore()

    def greet_dom(i, c):
        e = lax.rem(d + i, ND)
        pl.semaphore_signal(barrier, inc=1, device_id=(f, e), device_id_type=MESH)
        return c

    def greet_feat(i, c):
        g = lax.rem(f + i, NF)
        pl.semaphore_signal(barrier, inc=1, device_id=(g, d), device_id_type=MESH)
        return c

    lax.fori_loop(1, ND, greet_dom, 0)
    lax.fori_loop(1, NF, greet_feat, 0)

    def tile_copy(i):
        part = pl.ds(i * STEP, STEP)
        return pltpu.make_async_copy(tiles_ref.at[0, part], wbuf.at[part], tile_sem.at[i])

    def start_tiles(i, c):
        tile_copy(i).start()
        return c

    lax.fori_loop(0, TILES // STEP, start_tiles, 0)
    grad_copy = pltpu.make_async_copy(grad_ref, gbuf, local_sem.at[0])
    grad_copy.start()

    for load in loads:
        load.wait()
    for h in range(2):
        for b in range(RB):
            block = feat_ref[h * HALF : (h + 1) * HALF, b * BLK : (b + 1) * BLK]
            own[h, b] = block
            slots[h, b] = block
            ffull[h, f, b] = block
        own[h, RB] = jnp.zeros((HALF, BLK), BF)

    def fill(e, c):
        count = counts_ref[0, e]
        for k in range(BMAX):
            pick = jnp.where(k < count, blocks_ref[0, k, e], RB)
            for h in range(2):
                sendbuf[h, e, k] = own[h, pick]
        return c

    lax.fori_loop(0, ND, fill, 0)
    for h in range(2):
        slots[h, pl.ds(RB + BMAX * d, BMAX)] = sendbuf[h, d]

    for g in range(NF):
        wsend[g] = jnp.concatenate(
            [sw_ref[:, g * HU : (g + 1) * HU], nw_ref[:, g * HU : (g + 1) * HU]], axis=1
        )
    wfull[f] = wsend[f]

    pl.semaphore_wait(barrier, ND - 1 + NF - 1)

    x, y, k = d // 8, lax.rem(d // 2, 4), lax.rem(d, 2)

    def plane_peer(p):
        return (lax.rem(x + p[0], 4) * 4 + lax.rem(y + p[1], 4)) * 2 + lax.rem(k + p[2], 2)

    def remote(source, held, stage, device):
        return pltpu.make_async_remote_copy(
            src_ref=source,
            dst_ref=held,
            send_sem=send_sem.at[stage],
            recv_sem=recv_sem.at[stage],
            device_id=device,
            device_id_type=MESH,
        )

    place = x
    shift = k * (7 - y) + (1 - k) * lax.rem(y + 1, 4)
    plane = lax.rem(f + shift, NF)

    def settle(ref, sem):
        pltpu.make_async_copy(ref, ref, sem).wait()

    boundary = pl.ds(RB + BMAX * d, BMAX)
    for h in range(2):
        for p in OTHERS:
            e = plane_peer(p)
            remote(sendbuf.at[h, e], slots.at[h, boundary], h, (f, e)).start()
    for i in COLUMN:
        g = lax.rem(f + i, NF)
        remote(wsend.at[g], wfull.at[f], 2, (g, d)).start()
    for i in COLUMN:
        g = lax.rem(f + i, NF)
        remote(own.at[:, pl.ds(0, RB)], ffull.at[:, f], 3, (g, d)).start()

    row = lax.broadcasted_iota(jnp.int32, (MROWS, BLK), 0)
    top = lax.broadcasted_iota(jnp.int32, (FR, BLK), 0)
    for j in range(RB):
        mask[j] = jnp.where((row >= HALF * j) & (row < HALF * (j + 1)), 1.0, 0.0).astype(BF)
        rowmask[j] = jnp.where(top == j, 1.0, 0.0).astype(BF)
    mask[RB] = jnp.zeros((MROWS, BLK), BF)
    rowmask[RB] = jnp.zeros((FR, BLK), BF)
    live = live_ref[0, 0]

    def goal(t):
        return jnp.where(t < live, target_ref[0, t], RB)

    def degree_step(i, total):
        tile_copy(i).wait()
        left = [rowmask[goal(i * STEP + u)] for u in range(STEP)]
        right = [wbuf[i * STEP + u] for u in range(STEP)]
        return total + dot_nt(jnp.concatenate(left, axis=1), jnp.concatenate(right, axis=1))

    degrees = lax.fori_loop(0, TILES // STEP, degree_step, jnp.zeros((FR, BLK), F32))
    inverse = 1.0 / (1.0 + degrees)

    wide = jnp.broadcast_to(bias_ref[...].reshape(1, HU), (BLK, HU))
    wide = jnp.concatenate([wide, jnp.zeros((BLK, BLK - HU), F32)], axis=1)
    bias_cols = jnp.transpose(wide)[:HU]

    def aggregate(h, c):
        settle(slots.at[h, pl.ds(RB, BMAX * (ND - 1))], recv_sem.at[h])

        def double(i, c):
            for u in range(8):
                block = slots[h, i * 8 + u]
                twice[i * 8 + u, :HALF] = block
                twice[i * 8 + u, HALF:] = block
            return c

        lax.fori_loop(0, NS // 8, double, 0)

        def step(i, total):
            left, right = [], []
            for u in range(STEP):
                t = i * STEP + u
                chosen = twice[source_ref[0, t]]
                left.append(jnp.concatenate([chosen] * (RB // 2), axis=0) * mask[goal(t)])
                right.append(wbuf[t])
            return total + dot_nt(jnp.concatenate(left, axis=1), jnp.concatenate(right, axis=1))

        total = lax.fori_loop(0, TILES // STEP, step, jnp.zeros((MROWS, BLK), F32))
        for b in range(RB):
            block = total[b * HALF : (b + 1) * HALF].astype(BF)
            abuf[h, b] = block
            afull[h, f, b] = block
        for i in COLUMN:
            g = lax.rem(f + i, NF)
            remote(abuf.at[h], afull.at[h, f], 4 + h, (g, d)).start()
        return c

    lax.fori_loop(0, 2, aggregate, 0)

    settle(wfull.at[pl.ds(0, NF - 1)], recv_sem.at[2])
    settle(ffull.at[:, pl.ds(0, NF - 1)], recv_sem.at[3])
    wide = wfull[...].astype(F32)
    wide = jnp.concatenate(
        [wide[:, h * HALF : (h + 1) * HALF].reshape(NF * HALF, BLK) for h in range(2)], axis=0
    )
    wt[...] = jnp.transpose(wide).astype(BF)
    for b in range(RB):
        fb = ffull[:, :, b].reshape(NF * FR, BLK)
        ubuf[b] = dot_nn(wt[:HU], fb) + bias_cols
    grad_copy.wait()

    for h in range(2):
        settle(afull.at[h, pl.ds(0, NF - 1)], recv_sem.at[4 + h])

    gtotal = jnp.zeros((NF * FR, BLK), F32)
    btotal = jnp.zeros((HU, BLK), F32)
    nothing = jnp.zeros((HU, BLK), BF)
    for b in range(RB):
        fb = ffull[:, :, b].reshape(NF * FR, BLK)
        ab = afull[:, :, b].reshape(NF * FR, BLK)
        inv = inverse[b : b + 1]
        v = ubuf[b] + dot_nn(wt[HU:], ab) * inv
        v2 = v * v
        t = jnp.tanh(C0 * v * (1.0 + C1 * v2))
        half = 0.5 * (1.0 + t)
        hbuf[:, b * BLK : (b + 1) * BLK] = (v * half).astype(BF)
        slope = half + 0.5 * v * (1.0 - t * t) * (C0 * (1.0 + 3.0 * C1 * v2))
        grad = gbuf[:, b * BLK : (b + 1) * BLK].astype(F32) * slope
        btotal = btotal + grad
        narrow = grad.astype(BF)
        scaled = (grad * inv).astype(BF)
        right = jnp.concatenate(
            [
                jnp.concatenate([narrow, nothing], axis=1),
                jnp.concatenate([nothing, scaled], axis=1),
            ],
            axis=0,
        )
        gtotal = gtotal + dot_nt(jnp.concatenate([fb, ab], axis=1), right)
    hidden_copy = pltpu.make_async_copy(hbuf, hidden_ref, local_sem.at[1])
    hidden_copy.start()

    ones8 = jnp.ones((8, BLK), BF)
    brow = jnp.zeros((8, BLK), F32)
    for part in split3(btotal):
        brow = brow + dot_nt(ones8, jnp.concatenate([part, nothing], axis=0))
    for g in range(NF):
        away = lax.rem(g - f + NF, NF)
        odd = away // 4
        near = odd * (7 - away) + (1 - odd) * lax.rem(away + 3, 4)
        for q in range(PIECE):
            p = (q * 4 + near) * 2 + odd
            at = (q // 2) * NF * HALF + g * HALF + (q % 2) * PIECE
            gsend[p, :PIECE] = gtotal[at : at + PIECE]
            gsend[p, PIECE:] = brow[:PIECE]
    grecv[d] = gsend[d]
    for p in OTHERS:
        e = plane_peer(p)
        remote(gsend.at[e], grecv.at[d], 6, (f, e)).start()
    settle(grecv.at[pl.ds(0, ND - 1)], recv_sem.at[6])

    added = grecv[0]
    for e in range(1, ND):
        added = added + grecv[e]
    red[...] = added[:PIECE]
    biasv[...] = added[PIECE : PIECE + 1, :HU]
    bias_copy = pltpu.make_async_copy(biasv, biasg_ref, local_sem.at[11])
    bias_copy.start()

    for p in OTHERS:
        remote(red, fin.at[f, place], 7, (plane, plane_peer(p))).start()

    @pl.when(shift != 0)
    def _():
        remote(red, fin.at[f, place], 7, (plane, d)).start()

    @pl.when(shift == 0)
    def _():
        fin[f, place] = red[...]

    flat = fin.reshape(ND, PIECE, BLK)

    @pl.when(shift == 0)
    def _():
        settle(flat.at[pl.ds(0, ND - 1)], recv_sem.at[7])

    @pl.when(shift != 0)
    def _():
        settle(flat, recv_sem.at[7])

    rows = [jnp.concatenate([fin[g, q] for q in range(PIECE)], axis=0) for g in range(NF)]
    for j in range(0, NF, 2):
        a, b = rows[j], rows[j + 1]
        at = slice(j * HU, (j + 2) * HU)
        selfv[:, at] = jnp.concatenate([a[:, :HU], b[:, :HU]], axis=1)
        neighv[:, at] = jnp.concatenate([a[:, HU:], b[:, HU:]], axis=1)
    self_copy = pltpu.make_async_copy(selfv, selfg_ref, local_sem.at[12])
    self_copy.start()
    neigh_copy = pltpu.make_async_copy(neighv, neighg_ref, local_sem.at[13])
    neigh_copy.start()

    for h in range(2):
        settle(sendbuf.at[h, pl.ds(0, ND - 1)], send_sem.at[h])
        settle(afull.at[h, pl.ds(0, NF - 1)], send_sem.at[4 + h])
    settle(wsend.at[pl.ds(0, NF - 1)], send_sem.at[2])
    settle(ffull.at[:, pl.ds(0, NF - 1)], send_sem.at[3])
    settle(gsend.at[pl.ds(0, ND - 1)], send_sem.at[6])

    @pl.when(shift == 0)
    def _():
        settle(flat.at[pl.ds(0, ND - 1)], send_sem.at[7])

    @pl.when(shift != 0)
    def _():
        settle(flat, send_sem.at[7])

    for copy in (bias_copy, hidden_copy, self_copy, neigh_copy):
        copy.wait()


def hand_over(*refs):
    for made, out in zip(refs[:4], refs[4:]):
        out[...] = made[...]


def body(
    features,
    self_weight,
    neighbor_weight,
    unit_bias,
    send_blocks,
    send_counts,
    tile_target,
    tile_source,
    tile_count,
    tile_weights,
    out_grad,
):
    hbm = pl.BlockSpec(memory_space=pltpu.HBM)
    vmem = pl.BlockSpec(memory_space=pltpu.VMEM)
    shapes = (
        jax.ShapeDtypeStruct((HU, RB * BLK), BF),
        jax.ShapeDtypeStruct((FR, NF * HU), F32),
        jax.ShapeDtypeStruct((FR, NF * HU), F32),
        jax.ShapeDtypeStruct((1, HU), F32),
    )
    made = pl.pallas_call(
        kernel,
        out_shape=tuple(pltpu.VMEM(one.shape, one.dtype) for one in shapes),
        in_specs=[hbm] * 11,
        out_specs=(vmem,) * 4,
        scratch_shapes=[
            pltpu.VMEM((FR, RB * BLK), BF),
            pltpu.VMEM((FR, NF * HU), BF),
            pltpu.VMEM((FR, NF * HU), BF),
            pltpu.VMEM((HU,), F32),
            pltpu.SMEM((1, BMAX, ND), jnp.int32),
            pltpu.SMEM((1, ND), jnp.int32),
            pltpu.SMEM((1, TILES), jnp.int32),
            pltpu.SMEM((1, TILES), jnp.int32),
            pltpu.SMEM((1, 1), jnp.int32),
            pltpu.VMEM((2, RB + 1, HALF, BLK), BF),
            pltpu.VMEM((2, ND, BMAX, HALF, BLK), BF),
            pltpu.VMEM((2, NS, HALF, BLK), BF),
            pltpu.VMEM((NS, FR, BLK), BF),
            pltpu.VMEM((TILES, BLK, BLK), BF),
            pltpu.VMEM((RB + 1, MROWS, BLK), BF),
            pltpu.VMEM((RB + 1, FR, BLK), BF),
            pltpu.VMEM((2, NF, RB, HALF, BLK), BF),
            pltpu.VMEM((NF, FR, BLK), BF),
            pltpu.VMEM((NF, FR, BLK), BF),
            pltpu.VMEM((BLK, NF * FR), BF),
            pltpu.VMEM((2, RB, HALF, BLK), BF),
            pltpu.VMEM((2, NF, RB, HALF, BLK), BF),
            pltpu.VMEM((RB, HU, BLK), F32),
            pltpu.VMEM((HU, RB * BLK), BF),
            pltpu.VMEM((HU, RB * BLK), BF),
            pltpu.VMEM((ND, 8, BLK), F32),
            pltpu.VMEM((ND, 8, BLK), F32),
            pltpu.VMEM((PIECE, BLK), F32),
            pltpu.VMEM((NF, PIECE, PIECE, BLK), F32),
            pltpu.VMEM((FR, NF * HU), F32),
            pltpu.VMEM((FR, NF * HU), F32),
            pltpu.VMEM((1, HU), F32),
            pltpu.SemaphoreType.DMA((TILES // STEP,)),
            pltpu.SemaphoreType.DMA((14,)),
            pltpu.SemaphoreType.DMA((8,)),
            pltpu.SemaphoreType.DMA((8,)),
        ],
        compiler_params=pltpu.CompilerParams(
            collective_id=0, has_side_effects=True, vmem_limit_bytes=60 << 20
        ),
    )(
        features,
        self_weight,
        neighbor_weight,
        unit_bias,
        jnp.transpose(send_blocks, (0, 2, 1)),
        send_counts,
        tile_target,
        tile_source,
        tile_count.reshape(1, 1),
        tile_weights,
        out_grad,
    )
    hidden, selfg, neighg, biasg = pl.pallas_call(
        hand_over,
        out_shape=shapes,
        in_specs=[vmem] * 4,
        out_specs=(vmem,) * 4,
    )(*[pltpu.with_memory_space_constraint(one, pltpu.VMEM) for one in made])
    return hidden, selfg, neighg, biasg.reshape(HU)


def solution(mesh):
    in_specs = (
        P("feat", "dom"),
        P("feat", None),
        P("feat", None),
        P("feat"),
        P("dom", None, None),
        P("dom", None),
        P("dom", None),
        P("dom", None),
        P("dom"),
        P("dom", None, None, None),
        P("feat", "dom"),
    )
    out_specs = (P("feat", "dom"), P("feat", None), P("feat", None), P("feat"))
    return jax.shard_map(body, mesh=mesh, in_specs=in_specs, out_specs=out_specs, check_vma=False)
```

```python
import functools

import jax
import jax.numpy as jnp
from jax import lax
from jax.experimental import pallas as pl
from jax.experimental.pallas import tpu as pltpu
from jax.sharding import PartitionSpec as P

BLK = 128
BMAX = 4
NF = 8
ND = 32
RB = 8
NS = 136
TILES = 256
STEP = 32
LONG = 256
FR = 16
HU = 64
PIECE = 4
HALF = FR // 2
MROWS = RB * HALF


def around(n, i):
    return min(i, n - i)


PLANE = sorted(
    ((x, y, c) for x in range(4) for y in range(4) for c in range(2)),
    key=lambda p: (-around(4, p[0]) - around(4, p[1]), -p[2]),
)
COLUMN = sorted(range(1, NF), key=lambda z: -around(NF, z))


def step_of(t):
    return lax.rem(10 - t + (t // 2) * (3 + 2 * lax.rem(t, 2)), 4)


BF = jnp.bfloat16
F32 = jnp.float32
MESH = pl.DeviceIdType.MESH
C0 = 0.7978845608028654
C1 = 0.044715


def dot_nt(a, b):
    return lax.dot_general(a, b, (((1,), (1,)), ((), ())), preferred_element_type=F32)


def dot_nn(a, b):
    return lax.dot_general(a, b, (((1,), (0,)), ((), ())), preferred_element_type=F32)


def split3(x):
    hi = x.astype(BF)
    rest = x - hi.astype(F32)
    mid = rest.astype(BF)
    low = (rest - mid.astype(F32)).astype(BF)
    return hi, mid, low


def kernel(
    feat_hbm,
    sw_hbm,
    nw_hbm,
    bias_hbm,
    blocks_hbm,
    counts_hbm,
    target_hbm,
    source_hbm,
    live_hbm,
    tiles_ref,
    grad_ref,
    hidden_ref,
    selfg_ref,
    neighg_ref,
    biasg_ref,
    feat_ref,
    sw_ref,
    nw_ref,
    bias_ref,
    blocks_ref,
    counts_ref,
    target_ref,
    source_ref,
    live_ref,
    own,
    sendbuf,
    slots,
    twice,
    wbuf,
    mask,
    inverse,
    ffull,
    wsend,
    wfull,
    wt,
    abuf,
    afull,
    ubuf,
    vbuf,
    narrow,
    scaled,
    gscratch,
    gbuf,
    gsend,
    grecv,
    red,
    fin,
    tile_sem,
    local_sem,
    send_sem,
    recv_sem,
):
    f = lax.axis_index("feat")
    d = lax.axis_index("dom")

    x, y, k = d // 8, lax.rem(d // 2, 4), lax.rem(d, 2)

    def plane_peer(j):
        p = PLANE[j]
        return (lax.rem(x + p[0], 4) * 4 + lax.rem(y + p[1], 4)) * 2 + lax.rem(k + p[2], 2)

    def column_peer(i):
        return lax.rem(f + COLUMN[i], NF)

    def each(count, send):
        for i in range(count):
            send(i)

    barrier = pltpu.get_barrier_semaphore()
    for j in range(ND - 1):
        pl.semaphore_signal(barrier, inc=1, device_id=(f, plane_peer(j)), device_id_type=MESH)
    for i in range(NF - 1):
        pl.semaphore_signal(barrier, inc=1, device_id=(column_peer(i), d), device_id_type=MESH)

    loads = [
        pltpu.make_async_copy(source, held, local_sem.at[2 + i])
        for i, (source, held) in enumerate(
            [
                (feat_hbm, feat_ref),
                (counts_hbm, counts_ref),
                (blocks_hbm, blocks_ref),
                (sw_hbm, sw_ref),
                (nw_hbm, nw_ref),
                (bias_hbm, bias_ref),
                (target_hbm, target_ref),
                (source_hbm, source_ref),
                (live_hbm, live_ref),
            ]
        )
    ]
    for load in loads:
        load.start()
    def tile_copy(i):
        part = pl.ds(i * STEP, STEP)
        return pltpu.make_async_copy(tiles_ref.at[0, part], wbuf.at[part], tile_sem.at[i])

    def start_tiles(i, c):
        tile_copy(i).start()
        return c

    lax.fori_loop(0, TILES // STEP, start_tiles, 0)
    grad_copy = pltpu.make_async_copy(grad_ref, gbuf, local_sem.at[0])
    grad_copy.start()

    for load in loads:
        load.wait()
    for h in range(2):
        for b in range(RB):
            block = feat_ref[h * HALF : (h + 1) * HALF, b * BLK : (b + 1) * BLK]
            own[h, b] = block
            slots[h, b] = block
            ffull[h, f, b] = block
        own[h, RB] = jnp.zeros((HALF, BLK), BF)

    def fill(e, c):
        count = counts_ref[0, e]
        for k in range(BMAX):
            pick = jnp.where(k < count, blocks_ref[0, k, e], RB)
            for h in range(2):
                sendbuf[h, e, k] = own[h, pick]
        return c

    lax.fori_loop(0, ND, fill, 0)
    for h in range(2):
        slots[h, pl.ds(RB + BMAX * d, BMAX)] = sendbuf[h, d]

    for g in range(NF):
        wsend[g] = jnp.concatenate(
            [sw_ref[:, g * HU : (g + 1) * HU], nw_ref[:, g * HU : (g + 1) * HU]], axis=1
        )
    wfull[f] = wsend[f]

    pl.semaphore_wait(barrier, ND - 1 + NF - 1)

    def remote(source, held, stage, device):
        return pltpu.make_async_remote_copy(
            src_ref=source,
            dst_ref=held,
            send_sem=send_sem.at[stage],
            recv_sem=recv_sem.at[stage],
            device_id=device,
            device_id_type=MESH,
        )

    place = x
    shift = k * (7 - y) + (1 - k) * lax.rem(y + 1, 4)
    plane = lax.rem(f + shift, NF)

    def settle(ref, sem):
        pltpu.make_async_copy(ref, ref, sem).wait()

    boundary = pl.ds(RB + BMAX * d, BMAX)
    for h in range(2):

        def send_slots(j, h=h):
            e = plane_peer(j)
            remote(sendbuf.at[h, e], slots.at[h, boundary], h, (f, e)).start()

        each(ND - 1, send_slots)

    def send_inputs(i):
        g = column_peer(i)
        remote(wsend.at[g], wfull.at[f], 2, (g, d)).start()
        remote(own.at[:, pl.ds(0, RB)], ffull.at[:, f], 3, (g, d)).start()

    each(NF - 1, send_inputs)

    row = lax.broadcasted_iota(jnp.int32, (MROWS, BLK), 0)
    for j in range(RB):
        mask[j] = jnp.where((row >= HALF * j) & (row < HALF * (j + 1)), 1.0, 0.0).astype(BF)
    mask[RB] = jnp.zeros((MROWS, BLK), BF)
    live = live_ref[0, 0]

    def goal(t):
        return jnp.where(t < live, target_ref[0, t], RB)

    def fill_ones(i, c):
        twice[i] = jnp.ones((FR, BLK), BF)
        return c

    lax.fori_loop(0, NS, fill_ones, 0)

    wide = jnp.broadcast_to(bias_ref[...].reshape(1, HU), (BLK, HU))
    wide = jnp.concatenate([wide, jnp.zeros((BLK, BLK - HU), F32)], axis=1)
    bias_cols = jnp.transpose(wide)[:HU]

    def double(h, i, c):
        for u in range(8):
            block = slots[h, i * 8 + u]
            twice[i * 8 + u, :HALF] = block
            twice[i * 8 + u, HALF:] = block
        return c

    def aggregate(turn, c):
        h = turn - 1

        @pl.when(turn == 0)
        def _():
            for i in range(TILES // STEP):
                tile_copy(i).wait()

        @pl.when(turn > 0)
        def _():
            settle(slots.at[h, pl.ds(RB, BMAX * (ND - 1))], recv_sem.at[h])
            lax.fori_loop(0, NS // 8, functools.partial(double, h), 0)

        def step(i, total):
            left, right = [], []
            for u in range(LONG):
                t = i * LONG + u
                chosen = twice[source_ref[0, t]]
                left.append(jnp.concatenate([chosen] * (RB // 2), axis=0) * mask[goal(t)])
                right.append(wbuf[t])
            return total + dot_nt(jnp.concatenate(left, axis=1), jnp.concatenate(right, axis=1))

        total = lax.fori_loop(0, TILES // LONG, step, jnp.zeros((MROWS, BLK), F32))

        @pl.when(turn == 0)
        def _():
            inverse[...] = 1.0 / (1.0 + total)

        @pl.when(turn > 0)
        def _():
            for b in range(RB):
                block = total[b * HALF : (b + 1) * HALF].astype(BF)
                abuf[h, b] = block
                afull[h, f, b] = block

            def send_aggregate(i):
                g = column_peer(i)
                remote(abuf.at[h], afull.at[h, f], 4 + h, (g, d)).start()

            each(NF - 1, send_aggregate)

        return c

    lax.fori_loop(0, 3, aggregate, 0)

    settle(wfull.at[pl.ds(0, NF - 1)], recv_sem.at[2])
    settle(ffull.at[:, pl.ds(0, NF - 1)], recv_sem.at[3])
    wide = wfull[...].astype(F32)
    wide = jnp.concatenate(
        [wide[:, h * HALF : (h + 1) * HALF].reshape(NF * HALF, BLK) for h in range(2)], axis=0
    )
    wt[...] = jnp.transpose(wide).astype(BF)
    fblocks = [ffull[:, :, b].reshape(NF * FR, BLK) for b in range(RB)]
    uall = dot_nn(wt[:HU], jnp.concatenate(fblocks, axis=1))
    for b in range(RB):
        ubuf[b] = uall[:, b * BLK : (b + 1) * BLK] + bias_cols
    grad_copy.wait()

    for h in range(2):
        settle(afull.at[h, pl.ds(0, NF - 1)], recv_sem.at[4 + h])

    ablocks = [afull[:, :, b].reshape(NF * FR, BLK) for b in range(RB)]
    vall = dot_nn(wt[HU:], jnp.concatenate(ablocks, axis=1))
    for b in range(RB):
        vbuf[b] = vall[:, b * BLK : (b + 1) * BLK]
    nothing = jnp.zeros((HU, BLK), BF)

    def activate(b, btotal):
        at = pl.ds(pl.multiple_of(b * BLK, BLK), BLK)
        inv = inverse[pl.ds(pl.multiple_of(b * HALF, HALF), HALF)][:1]
        v = ubuf[b] + vbuf[b] * inv
        v2 = v * v
        t = jnp.tanh(C0 * v * (1.0 + C1 * v2))
        half = 0.5 * (1.0 + t)
        hidden_ref[:, at] = (v * half).astype(BF)
        slope = half + 0.5 * v * (1.0 - t * t) * (C0 * (1.0 + 3.0 * C1 * v2))
        grad = gbuf[:, at].astype(F32) * slope
        narrow[b] = grad.astype(BF)
        scaled[b] = (grad * inv).astype(BF)
        return btotal + grad

    btotal = lax.fori_loop(0, RB, activate, jnp.zeros((HU, BLK), F32), unroll=True)
    lefts, rights = [], []
    for b in range(RB):
        lefts += [ffull[:, :, b].reshape(NF * FR, BLK), ablocks[b]]
        rights.append(
            jnp.concatenate(
                [
                    jnp.concatenate([narrow[b], nothing], axis=1),
                    jnp.concatenate([nothing, scaled[b]], axis=1),
                ],
                axis=0,
            )
        )
    gtotal = dot_nt(jnp.concatenate(lefts, axis=1), jnp.concatenate(rights, axis=1))
    gscratch[...] = gtotal.reshape(ND, PIECE, BLK)

    ones8 = jnp.ones((8, BLK), BF)
    brow = jnp.zeros((8, BLK), F32)
    for part in split3(btotal):
        brow = brow + dot_nt(ones8, jnp.concatenate([part, nothing], axis=0))
    def place_rows(g, c):
        away = lax.rem(g - f + NF, NF)
        odd = away // 4
        near = odd * (7 - away) + (1 - odd) * lax.rem(away + 3, 4)
        for q in range(PIECE):
            p = (q * 4 + near) * 2 + odd
            gsend[p, :PIECE] = gscratch[(q // 2) * 2 * NF + g * 2 + q % 2]
            gsend[p, PIECE:] = brow[:PIECE]
        return c

    lax.fori_loop(0, NF, place_rows, 0, unroll=True)
    grecv[d] = gsend[d]
    def send_parts(j):
        e = plane_peer(j)
        remote(gsend.at[e], grecv.at[d], 6, (f, e)).start()

    each(ND - 1, send_parts)
    settle(grecv.at[pl.ds(0, ND - 1)], recv_sem.at[6])

    added = grecv[0]
    for e in range(1, ND):
        added = added + grecv[e]
    red[...] = added[:PIECE]
    biasg_ref[...] = added[PIECE : PIECE + 1, :HU]

    def send_rows(j):
        remote(red, fin.at[f, place], 7, (plane, plane_peer(j))).start()

    each(ND - 1, send_rows)

    @pl.when(shift != 0)
    def _():
        send_rows(ND - 1)

    @pl.when(shift == 0)
    def _():
        fin[f, place] = red[...]

    flat = fin.reshape(ND, PIECE, BLK)

    @pl.when(shift == 0)
    def _():
        settle(flat.at[pl.ds(0, ND - 1)], recv_sem.at[7])

    @pl.when(shift != 0)
    def _():
        settle(flat, recv_sem.at[7])

    def assemble(j, c):
        a, b = [
            jnp.concatenate([fin[2 * j + i, q] for q in range(PIECE)], axis=0) for i in range(2)
        ]
        at = pl.ds(pl.multiple_of(j * BLK, BLK), BLK)
        selfg_ref[:, at] = jnp.concatenate([a[:, :HU], b[:, :HU]], axis=1)
        neighg_ref[:, at] = jnp.concatenate([a[:, HU:], b[:, HU:]], axis=1)
        return c

    lax.fori_loop(0, NF // 2, assemble, 0, unroll=True)

    for h in range(2):
        settle(sendbuf.at[h, pl.ds(0, ND - 1)], send_sem.at[h])
        settle(afull.at[h, pl.ds(0, NF - 1)], send_sem.at[4 + h])
    settle(wsend.at[pl.ds(0, NF - 1)], send_sem.at[2])
    settle(ffull.at[:, pl.ds(0, NF - 1)], send_sem.at[3])
    settle(gsend.at[pl.ds(0, ND - 1)], send_sem.at[6])

    @pl.when(shift == 0)
    def _():
        settle(flat.at[pl.ds(0, ND - 1)], send_sem.at[7])

    @pl.when(shift != 0)
    def _():
        settle(flat, send_sem.at[7])


def hand_over(*refs):
    for made, out in zip(refs[:4], refs[4:]):
        out[...] = made[...]


def body(
    features,
    self_weight,
    neighbor_weight,
    unit_bias,
    send_blocks,
    send_counts,
    tile_target,
    tile_source,
    tile_count,
    tile_weights,
    out_grad,
):
    hbm = pl.BlockSpec(memory_space=pltpu.HBM)
    vmem = pl.BlockSpec(memory_space=pltpu.VMEM)
    shapes = (
        jax.ShapeDtypeStruct((HU, RB * BLK), BF),
        jax.ShapeDtypeStruct((FR, NF * HU), F32),
        jax.ShapeDtypeStruct((FR, NF * HU), F32),
        jax.ShapeDtypeStruct((1, HU), F32),
    )
    made = pl.pallas_call(
        kernel,
        out_shape=tuple(pltpu.VMEM(one.shape, one.dtype) for one in shapes),
        in_specs=[hbm] * 11,
        out_specs=(vmem,) * 4,
        scratch_shapes=[
            pltpu.VMEM((FR, RB * BLK), BF),
            pltpu.VMEM((FR, NF * HU), BF),
            pltpu.VMEM((FR, NF * HU), BF),
            pltpu.VMEM((HU,), F32),
            pltpu.SMEM((1, BMAX, ND), jnp.int32),
            pltpu.SMEM((1, ND), jnp.int32),
            pltpu.SMEM((1, TILES), jnp.int32),
            pltpu.SMEM((1, TILES), jnp.int32),
            pltpu.SMEM((1, 1), jnp.int32),
            pltpu.VMEM((2, RB + 1, HALF, BLK), BF),
            pltpu.VMEM((2, ND, BMAX, HALF, BLK), BF),
            pltpu.VMEM((2, NS, HALF, BLK), BF),
            pltpu.VMEM((NS, FR, BLK), BF),
            pltpu.VMEM((TILES, BLK, BLK), BF),
            pltpu.VMEM((RB + 1, MROWS, BLK), BF),
            pltpu.VMEM((MROWS, BLK), F32),
            pltpu.VMEM((2, NF, RB, HALF, BLK), BF),
            pltpu.VMEM((NF, FR, BLK), BF),
            pltpu.VMEM((NF, FR, BLK), BF),
            pltpu.VMEM((BLK, NF * FR), BF),
            pltpu.VMEM((2, RB, HALF, BLK), BF),
            pltpu.VMEM((2, NF, RB, HALF, BLK), BF),
            pltpu.VMEM((RB, HU, BLK), F32),
            pltpu.VMEM((RB, HU, BLK), F32),
            pltpu.VMEM((RB, HU, BLK), BF),
            pltpu.VMEM((RB, HU, BLK), BF),
            pltpu.VMEM((ND, PIECE, BLK), F32),
            pltpu.VMEM((HU, RB * BLK), BF),
            pltpu.VMEM((ND, 8, BLK), F32),
            pltpu.VMEM((ND, 8, BLK), F32),
            pltpu.VMEM((PIECE, BLK), F32),
            pltpu.VMEM((NF, PIECE, PIECE, BLK), F32),
            pltpu.SemaphoreType.DMA((TILES // STEP,)),
            pltpu.SemaphoreType.DMA((14,)),
            pltpu.SemaphoreType.DMA((8,)),
            pltpu.SemaphoreType.DMA((8,)),
        ],
        compiler_params=pltpu.CompilerParams(
            collective_id=0, has_side_effects=True, vmem_limit_bytes=60 << 20
        ),
    )(
        features,
        self_weight,
        neighbor_weight,
        unit_bias,
        jnp.transpose(send_blocks, (0, 2, 1)),
        send_counts,
        tile_target,
        tile_source,
        tile_count.reshape(1, 1),
        tile_weights,
        out_grad,
    )
    hidden, selfg, neighg, biasg = pl.pallas_call(
        hand_over,
        out_shape=shapes,
        in_specs=[vmem] * 4,
        out_specs=(vmem,) * 4,
    )(*[pltpu.with_memory_space_constraint(one, pltpu.VMEM) for one in made])
    return hidden, selfg, neighg, biasg.reshape(HU)


def solution(mesh):
    in_specs = (
        P("feat", "dom"),
        P("feat", None),
        P("feat", None),
        P("feat"),
        P("dom", None, None),
        P("dom", None),
        P("dom", None),
        P("dom", None),
        P("dom"),
        P("dom", None, None, None),
        P("feat", "dom"),
    )
    out_specs = (P("feat", "dom"), P("feat", None), P("feat", None), P("feat"))
    return jax.shard_map(body, mesh=mesh, in_specs=in_specs, out_specs=out_specs, check_vma=False)
```

```python
import functools

import jax
import jax.numpy as jnp
from jax import lax
from jax.experimental import pallas as pl
from jax.experimental.pallas import tpu as pltpu
from jax.sharding import PartitionSpec as P

BLK = 128
BMAX = 4
NF = 8
ND = 32
RB = 8
NS = 136
TILES = 256
STEP = 32
LONG = 128
FR = 16
HU = 64
PIECE = 4
HALF = FR // 2
MROWS = RB * FR


def around(n, i):
    return min(i, n - i)


PLANE = sorted(
    ((x, y, c) for x in range(4) for y in range(4) for c in range(2)),
    key=lambda p: (-around(4, p[0]) - around(4, p[1]), -p[2]),
)
COLUMN = sorted(range(1, NF), key=lambda z: -around(NF, z))


def step_of(t):
    return lax.rem(10 - t + (t // 2) * (3 + 2 * lax.rem(t, 2)), 4)


BF = jnp.bfloat16
F32 = jnp.float32
MESH = pl.DeviceIdType.MESH
C0 = 0.7978845608028654
C1 = 0.044715


def dot_nt(a, b):
    return lax.dot_general(a, b, (((1,), (1,)), ((), ())), preferred_element_type=F32)


def dot_nn(a, b):
    return lax.dot_general(a, b, (((1,), (0,)), ((), ())), preferred_element_type=F32)


def split3(x):
    hi = x.astype(BF)
    rest = x - hi.astype(F32)
    mid = rest.astype(BF)
    low = (rest - mid.astype(F32)).astype(BF)
    return hi, mid, low


def kernel(
    feat_hbm,
    sw_hbm,
    nw_hbm,
    bias_hbm,
    blocks_hbm,
    counts_hbm,
    target_hbm,
    source_hbm,
    live_hbm,
    tiles_ref,
    grad_ref,
    hidden_ref,
    selfg_ref,
    neighg_ref,
    biasg_ref,
    feat_ref,
    sw_ref,
    nw_ref,
    bias_ref,
    blocks_ref,
    counts_ref,
    target_ref,
    source_ref,
    live_ref,
    own,
    sendbuf,
    slots,
    padded,
    wbuf,
    mask,
    inverse,
    ffull,
    wsend,
    wfull,
    wt,
    abuf,
    afull,
    ubuf,
    vbuf,
    narrow,
    scaled,
    gscratch,
    gbuf,
    gsend,
    grecv,
    red,
    fin,
    tile_sem,
    local_sem,
    send_sem,
    recv_sem,
):
    f = lax.axis_index("feat")
    d = lax.axis_index("dom")

    x, y, k = d // 8, lax.rem(d // 2, 4), lax.rem(d, 2)

    def plane_peer(j):
        p = PLANE[j]
        return (lax.rem(x + p[0], 4) * 4 + lax.rem(y + p[1], 4)) * 2 + lax.rem(k + p[2], 2)

    def column_peer(i):
        return lax.rem(f + COLUMN[i], NF)

    def each(count, send):
        for i in range(count):
            send(i)

    barrier = pltpu.get_barrier_semaphore()
    for j in range(ND - 1):
        pl.semaphore_signal(barrier, inc=1, device_id=(f, plane_peer(j)), device_id_type=MESH)
    for i in range(NF - 1):
        pl.semaphore_signal(barrier, inc=1, device_id=(column_peer(i), d), device_id_type=MESH)

    loads = [
        pltpu.make_async_copy(source, held, local_sem.at[2 + i])
        for i, (source, held) in enumerate(
            [
                (feat_hbm, feat_ref),
                (counts_hbm, counts_ref),
                (blocks_hbm, blocks_ref),
                (sw_hbm, sw_ref),
                (nw_hbm, nw_ref),
                (bias_hbm, bias_ref),
                (target_hbm, target_ref),
                (source_hbm, source_ref),
                (live_hbm, live_ref),
            ]
        )
    ]
    for load in loads:
        load.start()
    def tile_copy(i):
        part = pl.ds(i * STEP, STEP)
        return pltpu.make_async_copy(tiles_ref.at[0, part], wbuf.at[part], tile_sem.at[i])

    def start_tiles(i, c):
        tile_copy(i).start()
        return c

    lax.fori_loop(0, TILES // STEP, start_tiles, 0)
    grad_copy = pltpu.make_async_copy(grad_ref, gbuf, local_sem.at[0])
    grad_copy.start()

    for load in loads:
        load.wait()
    for h in range(2):
        for b in range(RB):
            block = feat_ref[h * HALF : (h + 1) * HALF, b * BLK : (b + 1) * BLK]
            own[h, b] = block
            slots[h, b] = block
            ffull[h, f, b] = block
        own[h, RB] = jnp.zeros((HALF, BLK), BF)

    def fill(e, c):
        count = counts_ref[0, e]
        for k in range(BMAX):
            pick = jnp.where(k < count, blocks_ref[0, k, e], RB)
            for h in range(2):
                sendbuf[h, e, k] = own[h, pick]
        return c

    lax.fori_loop(0, ND, fill, 0)
    for h in range(2):
        slots[h, pl.ds(RB + BMAX * d, BMAX)] = sendbuf[h, d]

    for g in range(NF):
        wsend[g] = jnp.concatenate(
            [sw_ref[:, g * HU : (g + 1) * HU], nw_ref[:, g * HU : (g + 1) * HU]], axis=1
        )
    wfull[f] = wsend[f]

    pl.semaphore_wait(barrier, ND - 1 + NF - 1)

    def remote(source, held, stage, device):
        return pltpu.make_async_remote_copy(
            src_ref=source,
            dst_ref=held,
            send_sem=send_sem.at[stage],
            recv_sem=recv_sem.at[stage],
            device_id=device,
            device_id_type=MESH,
        )

    place = x
    shift = k * (7 - y) + (1 - k) * lax.rem(y + 1, 4)
    plane = lax.rem(f + shift, NF)

    def settle(ref, sem):
        pltpu.make_async_copy(ref, ref, sem).wait()

    boundary = pl.ds(RB + BMAX * d, BMAX)
    for h in range(2):

        def send_slots(j, h=h):
            e = plane_peer(j)
            remote(sendbuf.at[h, e], slots.at[h, boundary], h, (f, e)).start()

        each(ND - 1, send_slots)

    def send_inputs(i):
        g = column_peer(i)
        remote(wsend.at[g], wfull.at[f], 2, (g, d)).start()
        remote(own.at[:, pl.ds(0, RB)], ffull.at[:, f], 3, (g, d)).start()

    each(NF - 1, send_inputs)

    row = lax.broadcasted_iota(jnp.int32, (MROWS, BLK), 0)
    for j in range(RB):
        mask[j] = jnp.where((row >= FR * j) & (row < FR * (j + 1)), 1.0, 0.0).astype(BF)
    mask[RB] = jnp.zeros((MROWS, BLK), BF)
    live = live_ref[0, 0]

    def goal(t):
        return jnp.where(t < live, target_ref[0, t], RB)

    def fill_ones(i, c):
        padded[i] = jnp.ones((FR, BLK), BF)
        return c

    lax.fori_loop(0, NS, fill_ones, 0)

    wide = jnp.broadcast_to(bias_ref[...].reshape(1, HU), (BLK, HU))
    wide = jnp.concatenate([wide, jnp.zeros((BLK, BLK - HU), F32)], axis=1)
    bias_cols = jnp.transpose(wide)[:HU]

    def pad(h, i, c):
        for u in range(8):
            padded[i * 8 + u, :HALF] = slots[h, i * 8 + u]
        return c

    def aggregate(turn, c):
        h = turn - 1

        @pl.when(turn == 0)
        def _():
            for i in range(TILES // STEP):
                tile_copy(i).wait()

        @pl.when(turn > 0)
        def _():
            settle(slots.at[h, pl.ds(RB, BMAX * (ND - 1))], recv_sem.at[h])
            lax.fori_loop(0, NS // 8, functools.partial(pad, h), 0)

        def step(i, total):
            left, right = [], []
            for u in range(LONG):
                t = i * LONG + u
                chosen = padded[source_ref[0, t]]
                left.append(jnp.concatenate([chosen] * RB, axis=0) * mask[goal(t)])
                right.append(wbuf[t])
            return total + dot_nt(jnp.concatenate(left, axis=1), jnp.concatenate(right, axis=1))

        total = lax.fori_loop(0, TILES // LONG, step, jnp.zeros((MROWS, BLK), F32))

        @pl.when(turn == 0)
        def _():
            inverse[...] = 1.0 / (1.0 + total)

        @pl.when(turn > 0)
        def _():
            for b in range(RB):
                block = total[b * FR : b * FR + HALF].astype(BF)
                abuf[h, b] = block
                afull[h, f, b] = block

            def send_aggregate(i):
                g = column_peer(i)
                remote(abuf.at[h], afull.at[h, f], 4 + h, (g, d)).start()

            each(NF - 1, send_aggregate)

        return c

    lax.fori_loop(0, 3, aggregate, 0)

    settle(wfull.at[pl.ds(0, NF - 1)], recv_sem.at[2])
    settle(ffull.at[:, pl.ds(0, NF - 1)], recv_sem.at[3])
    wide = wfull[...].astype(F32)
    wide = jnp.concatenate(
        [wide[:, h * HALF : (h + 1) * HALF].reshape(NF * HALF, BLK) for h in range(2)], axis=0
    )
    wt[...] = jnp.transpose(wide).astype(BF)
    fblocks = [ffull[:, :, b].reshape(NF * FR, BLK) for b in range(RB)]
    uall = dot_nn(wt[:HU], jnp.concatenate(fblocks, axis=1))
    for b in range(RB):
        ubuf[b] = uall[:, b * BLK : (b + 1) * BLK] + bias_cols
    grad_copy.wait()

    for h in range(2):
        settle(afull.at[h, pl.ds(0, NF - 1)], recv_sem.at[4 + h])

    ablocks = [afull[:, :, b].reshape(NF * FR, BLK) for b in range(RB)]
    vall = dot_nn(wt[HU:], jnp.concatenate(ablocks, axis=1))
    for b in range(RB):
        vbuf[b] = vall[:, b * BLK : (b + 1) * BLK]
    nothing = jnp.zeros((HU, BLK), BF)

    def activate(b, btotal):
        at = pl.ds(pl.multiple_of(b * BLK, BLK), BLK)
        inv = inverse[pl.ds(pl.multiple_of(b * FR, FR), HALF)][:1]
        v = ubuf[b] + vbuf[b] * inv
        v2 = v * v
        t = jnp.tanh(C0 * v * (1.0 + C1 * v2))
        half = 0.5 * (1.0 + t)
        hidden_ref[:, at] = (v * half).astype(BF)
        slope = half + 0.5 * v * (1.0 - t * t) * (C0 * (1.0 + 3.0 * C1 * v2))
        grad = gbuf[:, at].astype(F32) * slope
        narrow[b] = grad.astype(BF)
        scaled[b] = (grad * inv).astype(BF)
        return btotal + grad

    btotal = lax.fori_loop(0, RB, activate, jnp.zeros((HU, BLK), F32), unroll=True)
    lefts, rights = [], []
    for b in range(RB):
        lefts += [ffull[:, :, b].reshape(NF * FR, BLK), ablocks[b]]
        rights.append(
            jnp.concatenate(
                [
                    jnp.concatenate([narrow[b], nothing], axis=1),
                    jnp.concatenate([nothing, scaled[b]], axis=1),
                ],
                axis=0,
            )
        )
    gtotal = dot_nt(jnp.concatenate(lefts, axis=1), jnp.concatenate(rights, axis=1))
    gscratch[...] = gtotal.reshape(ND, PIECE, BLK)

    ones8 = jnp.ones((8, BLK), BF)
    brow = jnp.zeros((8, BLK), F32)
    for part in split3(btotal):
        brow = brow + dot_nt(ones8, jnp.concatenate([part, nothing], axis=0))
    def place_rows(g, c):
        away = lax.rem(g - f + NF, NF)
        odd = away // 4
        near = odd * (7 - away) + (1 - odd) * lax.rem(away + 3, 4)
        for q in range(PIECE):
            p = (q * 4 + near) * 2 + odd
            gsend[p, :PIECE] = gscratch[(q // 2) * 2 * NF + g * 2 + q % 2]
            gsend[p, PIECE:] = brow[:PIECE]
        return c

    lax.fori_loop(0, NF, place_rows, 0, unroll=True)
    grecv[d] = gsend[d]
    def send_parts(j):
        e = plane_peer(j)
        remote(gsend.at[e], grecv.at[d], 6, (f, e)).start()

    each(ND - 1, send_parts)
    settle(grecv.at[pl.ds(0, ND - 1)], recv_sem.at[6])

    added = grecv[0]
    for e in range(1, ND):
        added = added + grecv[e]
    red[...] = added[:PIECE]
    biasg_ref[...] = added[PIECE : PIECE + 1, :HU]

    def send_rows(j):
        remote(red, fin.at[f, place], 7, (plane, plane_peer(j))).start()

    each(ND - 1, send_rows)

    @pl.when(shift != 0)
    def _():
        send_rows(ND - 1)

    @pl.when(shift == 0)
    def _():
        fin[f, place] = red[...]

    flat = fin.reshape(ND, PIECE, BLK)

    @pl.when(shift == 0)
    def _():
        settle(flat.at[pl.ds(0, ND - 1)], recv_sem.at[7])

    @pl.when(shift != 0)
    def _():
        settle(flat, recv_sem.at[7])

    def assemble(j, c):
        a, b = [
            jnp.concatenate([fin[2 * j + i, q] for q in range(PIECE)], axis=0) for i in range(2)
        ]
        at = pl.ds(pl.multiple_of(j * BLK, BLK), BLK)
        selfg_ref[:, at] = jnp.concatenate([a[:, :HU], b[:, :HU]], axis=1)
        neighg_ref[:, at] = jnp.concatenate([a[:, HU:], b[:, HU:]], axis=1)
        return c

    lax.fori_loop(0, NF // 2, assemble, 0, unroll=True)

    for h in range(2):
        settle(sendbuf.at[h, pl.ds(0, ND - 1)], send_sem.at[h])
        settle(afull.at[h, pl.ds(0, NF - 1)], send_sem.at[4 + h])
    settle(wsend.at[pl.ds(0, NF - 1)], send_sem.at[2])
    settle(ffull.at[:, pl.ds(0, NF - 1)], send_sem.at[3])
    settle(gsend.at[pl.ds(0, ND - 1)], send_sem.at[6])

    @pl.when(shift == 0)
    def _():
        settle(flat.at[pl.ds(0, ND - 1)], send_sem.at[7])

    @pl.when(shift != 0)
    def _():
        settle(flat, send_sem.at[7])


def hand_over(*refs):
    for made, out in zip(refs[:4], refs[4:]):
        out[...] = made[...]


def body(
    features,
    self_weight,
    neighbor_weight,
    unit_bias,
    send_blocks,
    send_counts,
    tile_target,
    tile_source,
    tile_count,
    tile_weights,
    out_grad,
):
    hbm = pl.BlockSpec(memory_space=pltpu.HBM)
    vmem = pl.BlockSpec(memory_space=pltpu.VMEM)
    shapes = (
        jax.ShapeDtypeStruct((HU, RB * BLK), BF),
        jax.ShapeDtypeStruct((FR, NF * HU), F32),
        jax.ShapeDtypeStruct((FR, NF * HU), F32),
        jax.ShapeDtypeStruct((1, HU), F32),
    )
    made = pl.pallas_call(
        kernel,
        out_shape=tuple(pltpu.VMEM(one.shape, one.dtype) for one in shapes),
        in_specs=[hbm] * 11,
        out_specs=(vmem,) * 4,
        scratch_shapes=[
            pltpu.VMEM((FR, RB * BLK), BF),
            pltpu.VMEM((FR, NF * HU), BF),
            pltpu.VMEM((FR, NF * HU), BF),
            pltpu.VMEM((HU,), F32),
            pltpu.SMEM((1, BMAX, ND), jnp.int32),
            pltpu.SMEM((1, ND), jnp.int32),
            pltpu.SMEM((1, TILES), jnp.int32),
            pltpu.SMEM((1, TILES), jnp.int32),
            pltpu.SMEM((1, 1), jnp.int32),
            pltpu.VMEM((2, RB + 1, HALF, BLK), BF),
            pltpu.VMEM((2, ND, BMAX, HALF, BLK), BF),
            pltpu.VMEM((2, NS, HALF, BLK), BF),
            pltpu.VMEM((NS, FR, BLK), BF),
            pltpu.VMEM((TILES, BLK, BLK), BF),
            pltpu.VMEM((RB + 1, MROWS, BLK), BF),
            pltpu.VMEM((MROWS, BLK), F32),
            pltpu.VMEM((2, NF, RB, HALF, BLK), BF),
            pltpu.VMEM((NF, FR, BLK), BF),
            pltpu.VMEM((NF, FR, BLK), BF),
            pltpu.VMEM((BLK, NF * FR), BF),
            pltpu.VMEM((2, RB, HALF, BLK), BF),
            pltpu.VMEM((2, NF, RB, HALF, BLK), BF),
            pltpu.VMEM((RB, HU, BLK), F32),
            pltpu.VMEM((RB, HU, BLK), F32),
            pltpu.VMEM((RB, HU, BLK), BF),
            pltpu.VMEM((RB, HU, BLK), BF),
            pltpu.VMEM((ND, PIECE, BLK), F32),
            pltpu.VMEM((HU, RB * BLK), BF),
            pltpu.VMEM((ND, 8, BLK), F32),
            pltpu.VMEM((ND, 8, BLK), F32),
            pltpu.VMEM((PIECE, BLK), F32),
            pltpu.VMEM((NF, PIECE, PIECE, BLK), F32),
            pltpu.SemaphoreType.DMA((TILES // STEP,)),
            pltpu.SemaphoreType.DMA((14,)),
            pltpu.SemaphoreType.DMA((8,)),
            pltpu.SemaphoreType.DMA((8,)),
        ],
        compiler_params=pltpu.CompilerParams(
            collective_id=0, has_side_effects=True, vmem_limit_bytes=60 << 20
        ),
    )(
        features,
        self_weight,
        neighbor_weight,
        unit_bias,
        jnp.transpose(send_blocks, (0, 2, 1)),
        send_counts,
        tile_target,
        tile_source,
        tile_count.reshape(1, 1),
        tile_weights,
        out_grad,
    )
    hidden, selfg, neighg, biasg = pl.pallas_call(
        hand_over,
        out_shape=shapes,
        in_specs=[vmem] * 4,
        out_specs=(vmem,) * 4,
    )(*[pltpu.with_memory_space_constraint(one, pltpu.VMEM) for one in made])
    return hidden, selfg, neighg, biasg.reshape(HU)


def solution(mesh):
    in_specs = (
        P("feat", "dom"),
        P("feat", None),
        P("feat", None),
        P("feat"),
        P("dom", None, None),
        P("dom", None),
        P("dom", None),
        P("dom", None),
        P("dom"),
        P("dom", None, None, None),
        P("feat", "dom"),
    )
    out_specs = (P("feat", "dom"), P("feat", None), P("feat", None), P("feat"))
    return jax.shard_map(body, mesh=mesh, in_specs=in_specs, out_specs=out_specs, check_vma=False)
```

```python
import functools

import jax
import jax.numpy as jnp
from jax import lax
from jax.experimental import pallas as pl
from jax.experimental.pallas import tpu as pltpu
from jax.sharding import PartitionSpec as P

BLK = 128
BMAX = 4
NF = 8
ND = 32
RB = 8
NS = 136
TILES = 256
STEP = 32
LONG = 128
FR = 16
HU = 64
PIECE = 4
HALF = FR // 2
MROWS = RB * FR


def around(n, i):
    return min(i, n - i)


PLANE = sorted(
    ((x, y, c) for x in range(4) for y in range(4) for c in range(2)),
    key=lambda p: (-around(4, p[0]) - around(4, p[1]), -p[2]),
)
COLUMN = sorted(range(1, NF), key=lambda z: -around(NF, z))


def step_of(t):
    return lax.rem(10 - t + (t // 2) * (3 + 2 * lax.rem(t, 2)), 4)


BF = jnp.bfloat16
F32 = jnp.float32
MESH = pl.DeviceIdType.MESH
C0 = 0.7978845608028654
C1 = 0.044715


def dot_nt(a, b):
    return lax.dot_general(a, b, (((1,), (1,)), ((), ())), preferred_element_type=F32)


def dot_nn(a, b):
    return lax.dot_general(a, b, (((1,), (0,)), ((), ())), preferred_element_type=F32)


def split3(x):
    hi = x.astype(BF)
    rest = x - hi.astype(F32)
    mid = rest.astype(BF)
    low = (rest - mid.astype(F32)).astype(BF)
    return hi, mid, low


def kernel(
    feat_hbm,
    sw_hbm,
    nw_hbm,
    bias_hbm,
    blocks_hbm,
    counts_hbm,
    target_hbm,
    source_hbm,
    live_hbm,
    tiles_ref,
    grad_ref,
    hidden_ref,
    selfg_ref,
    neighg_ref,
    biasg_ref,
    feat_ref,
    sw_ref,
    nw_ref,
    bias_ref,
    blocks_ref,
    counts_ref,
    target_ref,
    source_ref,
    live_ref,
    own,
    sendbuf,
    slots,
    padded,
    wbuf,
    mask,
    inverse,
    ffull,
    wsend,
    wfull,
    wt,
    abuf,
    afull,
    ubuf,
    vbuf,
    narrow,
    scaled,
    gscratch,
    gbuf,
    gsend,
    grecv,
    red,
    fin,
    tile_sem,
    local_sem,
    send_sem,
    recv_sem,
):
    f = lax.axis_index("feat")
    d = lax.axis_index("dom")

    x, y, k = d // 8, lax.rem(d // 2, 4), lax.rem(d, 2)

    def plane_peer(j):
        p = PLANE[j]
        return (lax.rem(x + p[0], 4) * 4 + lax.rem(y + p[1], 4)) * 2 + lax.rem(k + p[2], 2)

    def column_peer(i):
        return lax.rem(f + COLUMN[i], NF)

    def each(count, send):
        for i in range(count):
            send(i)

    barrier = pltpu.get_barrier_semaphore()
    for j in range(ND - 1):
        pl.semaphore_signal(barrier, inc=1, device_id=(f, plane_peer(j)), device_id_type=MESH)
    for i in range(NF - 1):
        pl.semaphore_signal(barrier, inc=1, device_id=(column_peer(i), d), device_id_type=MESH)

    loads = [
        pltpu.make_async_copy(source, held, local_sem.at[2 + i])
        for i, (source, held) in enumerate(
            [
                (feat_hbm, feat_ref),
                (counts_hbm, counts_ref),
                (blocks_hbm, blocks_ref),
                (sw_hbm, sw_ref),
                (nw_hbm, nw_ref),
                (bias_hbm, bias_ref),
                (target_hbm, target_ref),
                (source_hbm, source_ref),
                (live_hbm, live_ref),
            ]
        )
    ]
    for load in loads:
        load.start()
    def tile_copy(i):
        part = pl.ds(i * STEP, STEP)
        return pltpu.make_async_copy(tiles_ref.at[0, part], wbuf.at[part], tile_sem.at[i])

    def start_tiles(i, c):
        tile_copy(i).start()
        return c

    lax.fori_loop(0, TILES // STEP, start_tiles, 0)
    grad_copy = pltpu.make_async_copy(grad_ref, gbuf, local_sem.at[0])
    grad_copy.start()

    for load in loads:
        load.wait()
    for h in range(2):
        for b in range(RB):
            block = feat_ref[h * HALF : (h + 1) * HALF, b * BLK : (b + 1) * BLK]
            own[h, b] = block
            slots[h, b] = block
            ffull[h, f, b] = block
        own[h, RB] = jnp.zeros((HALF, BLK), BF)

    def fill(e, c):
        count = counts_ref[0, e]
        for k in range(BMAX):
            pick = jnp.where(k < count, blocks_ref[0, k, e], RB)
            for h in range(2):
                sendbuf[h, e, k] = own[h, pick]
        return c

    lax.fori_loop(0, ND, fill, 0)
    for h in range(2):
        slots[h, pl.ds(RB + BMAX * d, BMAX)] = sendbuf[h, d]

    for g in range(NF):
        wsend[g] = jnp.concatenate(
            [sw_ref[:, g * HU : (g + 1) * HU], nw_ref[:, g * HU : (g + 1) * HU]], axis=1
        )
    wfull[f] = wsend[f]

    pl.semaphore_wait(barrier, ND - 1 + NF - 1)

    def remote(source, held, stage, device):
        return pltpu.make_async_remote_copy(
            src_ref=source,
            dst_ref=held,
            send_sem=send_sem.at[stage],
            recv_sem=recv_sem.at[stage],
            device_id=device,
            device_id_type=MESH,
        )

    place = x
    shift = k * (7 - y) + (1 - k) * lax.rem(y + 1, 4)
    plane = lax.rem(f + shift, NF)

    def settle(ref, sem):
        pltpu.make_async_copy(ref, ref, sem).wait()

    boundary = pl.ds(RB + BMAX * d, BMAX)
    for h in range(2):

        def send_slots(j, h=h):
            e = plane_peer(j)
            remote(sendbuf.at[h, e], slots.at[h, boundary], h, (f, e)).start()

        each(ND - 1, send_slots)

    def send_inputs(i):
        g = column_peer(i)
        remote(wsend.at[g], wfull.at[f], 2, (g, d)).start()
        remote(own.at[:, pl.ds(0, RB)], ffull.at[:, f], 3, (g, d)).start()


    row = lax.broadcasted_iota(jnp.int32, (MROWS, BLK), 0)
    for j in range(RB):
        mask[j] = jnp.where((row >= FR * j) & (row < FR * (j + 1)), 1.0, 0.0).astype(BF)
    mask[RB] = jnp.zeros((MROWS, BLK), BF)
    live = live_ref[0, 0]

    def goal(t):
        return jnp.where(t < live, target_ref[0, t], RB)

    def fill_ones(i, c):
        padded[i] = jnp.ones((FR, BLK), BF)
        return c

    lax.fori_loop(0, NS, fill_ones, 0)

    wide = jnp.broadcast_to(bias_ref[...].reshape(1, HU), (BLK, HU))
    wide = jnp.concatenate([wide, jnp.zeros((BLK, BLK - HU), F32)], axis=1)
    bias_cols = jnp.transpose(wide)[:HU]

    def pad(h, i, c):
        for u in range(8):
            padded[i * 8 + u, :HALF] = slots[h, i * 8 + u]
        return c

    def aggregate(turn, c):
        h = turn - 1

        @pl.when(turn == 0)
        def _():
            for i in range(TILES // STEP):
                tile_copy(i).wait()

        @pl.when(turn > 0)
        def _():
            settle(slots.at[h, pl.ds(RB, BMAX * (ND - 1))], recv_sem.at[h])
            lax.fori_loop(0, NS // 8, functools.partial(pad, h), 0)

        def step(i, total):
            left, right = [], []
            for u in range(LONG):
                t = i * LONG + u
                chosen = padded[source_ref[0, t]]
                left.append(jnp.concatenate([chosen] * RB, axis=0) * mask[goal(t)])
                right.append(wbuf[t])
            return total + dot_nt(jnp.concatenate(left, axis=1), jnp.concatenate(right, axis=1))

        total = lax.fori_loop(0, TILES // LONG, step, jnp.zeros((MROWS, BLK), F32))

        @pl.when(turn == 0)
        def _():
            inverse[...] = 1.0 / (1.0 + total)
            each(NF - 1, send_inputs)

        @pl.when(turn > 0)
        def _():
            for b in range(RB):
                block = total[b * FR : b * FR + HALF].astype(BF)
                abuf[h, b] = block
                afull[h, f, b] = block

            def send_aggregate(i):
                g = column_peer(i)
                remote(abuf.at[h], afull.at[h, f], 4 + h, (g, d)).start()

            each(NF - 1, send_aggregate)

        return c

    lax.fori_loop(0, 3, aggregate, 0)

    settle(wfull.at[pl.ds(0, NF - 1)], recv_sem.at[2])
    settle(ffull.at[:, pl.ds(0, NF - 1)], recv_sem.at[3])
    wide = wfull[...].astype(F32)
    wide = jnp.concatenate(
        [wide[:, h * HALF : (h + 1) * HALF].reshape(NF * HALF, BLK) for h in range(2)], axis=0
    )
    wt[...] = jnp.transpose(wide).astype(BF)
    fblocks = [ffull[:, :, b].reshape(NF * FR, BLK) for b in range(RB)]
    uall = dot_nn(wt[:HU], jnp.concatenate(fblocks, axis=1))
    for b in range(RB):
        ubuf[b] = uall[:, b * BLK : (b + 1) * BLK] + bias_cols
    grad_copy.wait()

    for h in range(2):
        settle(afull.at[h, pl.ds(0, NF - 1)], recv_sem.at[4 + h])

    ablocks = [afull[:, :, b].reshape(NF * FR, BLK) for b in range(RB)]
    vall = dot_nn(wt[HU:], jnp.concatenate(ablocks, axis=1))
    for b in range(RB):
        vbuf[b] = vall[:, b * BLK : (b + 1) * BLK]
    nothing = jnp.zeros((HU, BLK), BF)

    def activate(b, btotal):
        at = pl.ds(pl.multiple_of(b * BLK, BLK), BLK)
        inv = inverse[pl.ds(pl.multiple_of(b * FR, FR), HALF)][:1]
        v = ubuf[b] + vbuf[b] * inv
        v2 = v * v
        t = jnp.tanh(C0 * v * (1.0 + C1 * v2))
        half = 0.5 * (1.0 + t)
        hidden_ref[:, at] = (v * half).astype(BF)
        slope = half + 0.5 * v * (1.0 - t * t) * (C0 * (1.0 + 3.0 * C1 * v2))
        grad = gbuf[:, at].astype(F32) * slope
        narrow[b] = grad.astype(BF)
        scaled[b] = (grad * inv).astype(BF)
        return btotal + grad

    btotal = lax.fori_loop(0, RB, activate, jnp.zeros((HU, BLK), F32), unroll=True)
    lefts, rights = [], []
    for b in range(RB):
        lefts += [ffull[:, :, b].reshape(NF * FR, BLK), ablocks[b]]
        rights.append(
            jnp.concatenate(
                [
                    jnp.concatenate([narrow[b], nothing], axis=1),
                    jnp.concatenate([nothing, scaled[b]], axis=1),
                ],
                axis=0,
            )
        )
    gtotal = dot_nt(jnp.concatenate(lefts, axis=1), jnp.concatenate(rights, axis=1))
    gscratch[...] = gtotal.reshape(ND, PIECE, BLK)

    terms = [jnp.concatenate([part, nothing], axis=0) for part in split3(btotal)]
    brow = dot_nt(jnp.ones((8, 3 * BLK), BF), jnp.concatenate(terms, axis=1))

    def place_rows(g, c):
        away = lax.rem(g - f + NF, NF)
        odd = away // 4
        near = odd * (7 - away) + (1 - odd) * lax.rem(away + 3, 4)
        for q in range(PIECE):
            p = (q * 4 + near) * 2 + odd
            gsend[p, :PIECE] = gscratch[(q // 2) * 2 * NF + g * 2 + q % 2]
            gsend[p, PIECE:] = brow[:PIECE]
        return c

    lax.fori_loop(0, NF, place_rows, 0, unroll=True)
    grecv[d] = gsend[d]
    def send_parts(j):
        e = plane_peer(j)
        remote(gsend.at[e], grecv.at[d], 6, (f, e)).start()

    each(ND - 1, send_parts)
    settle(grecv.at[pl.ds(0, ND - 1)], recv_sem.at[6])

    added = grecv[0]
    for e in range(1, ND):
        added = added + grecv[e]
    red[...] = added[:PIECE]
    biasg_ref[...] = added[PIECE : PIECE + 1, :HU]

    def send_rows(j):
        remote(red, fin.at[f, place], 7, (plane, plane_peer(j))).start()

    each(ND - 1, send_rows)

    @pl.when(shift != 0)
    def _():
        send_rows(ND - 1)

    @pl.when(shift == 0)
    def _():
        fin[f, place] = red[...]

    flat = fin.reshape(ND, PIECE, BLK)

    @pl.when(shift == 0)
    def _():
        settle(flat.at[pl.ds(0, ND - 1)], recv_sem.at[7])

    @pl.when(shift != 0)
    def _():
        settle(flat, recv_sem.at[7])

    def assemble(j, c):
        a, b = [
            jnp.concatenate([fin[2 * j + i, q] for q in range(PIECE)], axis=0) for i in range(2)
        ]
        at = pl.ds(pl.multiple_of(j * BLK, BLK), BLK)
        selfg_ref[:, at] = jnp.concatenate([a[:, :HU], b[:, :HU]], axis=1)
        neighg_ref[:, at] = jnp.concatenate([a[:, HU:], b[:, HU:]], axis=1)
        return c

    lax.fori_loop(0, NF // 2, assemble, 0, unroll=True)

    for h in range(2):
        settle(sendbuf.at[h, pl.ds(0, ND - 1)], send_sem.at[h])
        settle(afull.at[h, pl.ds(0, NF - 1)], send_sem.at[4 + h])
    settle(wsend.at[pl.ds(0, NF - 1)], send_sem.at[2])
    settle(ffull.at[:, pl.ds(0, NF - 1)], send_sem.at[3])
    settle(gsend.at[pl.ds(0, ND - 1)], send_sem.at[6])

    @pl.when(shift == 0)
    def _():
        settle(flat.at[pl.ds(0, ND - 1)], send_sem.at[7])

    @pl.when(shift != 0)
    def _():
        settle(flat, send_sem.at[7])


def hand_over(*refs):
    for made, out in zip(refs[:4], refs[4:]):
        out[...] = made[...]


def body(
    features,
    self_weight,
    neighbor_weight,
    unit_bias,
    send_blocks,
    send_counts,
    tile_target,
    tile_source,
    tile_count,
    tile_weights,
    out_grad,
):
    hbm = pl.BlockSpec(memory_space=pltpu.HBM)
    vmem = pl.BlockSpec(memory_space=pltpu.VMEM)
    shapes = (
        jax.ShapeDtypeStruct((HU, RB * BLK), BF),
        jax.ShapeDtypeStruct((FR, NF * HU), F32),
        jax.ShapeDtypeStruct((FR, NF * HU), F32),
        jax.ShapeDtypeStruct((1, HU), F32),
    )
    made = pl.pallas_call(
        kernel,
        out_shape=tuple(pltpu.VMEM(one.shape, one.dtype) for one in shapes),
        in_specs=[hbm] * 11,
        out_specs=(vmem,) * 4,
        scratch_shapes=[
            pltpu.VMEM((FR, RB * BLK), BF),
            pltpu.VMEM((FR, NF * HU), BF),
            pltpu.VMEM((FR, NF * HU), BF),
            pltpu.VMEM((HU,), F32),
            pltpu.SMEM((1, BMAX, ND), jnp.int32),
            pltpu.SMEM((1, ND), jnp.int32),
            pltpu.SMEM((1, TILES), jnp.int32),
            pltpu.SMEM((1, TILES), jnp.int32),
            pltpu.SMEM((1, 1), jnp.int32),
            pltpu.VMEM((2, RB + 1, HALF, BLK), BF),
            pltpu.VMEM((2, ND, BMAX, HALF, BLK), BF),
            pltpu.VMEM((2, NS, HALF, BLK), BF),
            pltpu.VMEM((NS, FR, BLK), BF),
            pltpu.VMEM((TILES, BLK, BLK), BF),
            pltpu.VMEM((RB + 1, MROWS, BLK), BF),
            pltpu.VMEM((MROWS, BLK), F32),
            pltpu.VMEM((2, NF, RB, HALF, BLK), BF),
            pltpu.VMEM((NF, FR, BLK), BF),
            pltpu.VMEM((NF, FR, BLK), BF),
            pltpu.VMEM((BLK, NF * FR), BF),
            pltpu.VMEM((2, RB, HALF, BLK), BF),
            pltpu.VMEM((2, NF, RB, HALF, BLK), BF),
            pltpu.VMEM((RB, HU, BLK), F32),
            pltpu.VMEM((RB, HU, BLK), F32),
            pltpu.VMEM((RB, HU, BLK), BF),
            pltpu.VMEM((RB, HU, BLK), BF),
            pltpu.VMEM((ND, PIECE, BLK), F32),
            pltpu.VMEM((HU, RB * BLK), BF),
            pltpu.VMEM((ND, 8, BLK), F32),
            pltpu.VMEM((ND, 8, BLK), F32),
            pltpu.VMEM((PIECE, BLK), F32),
            pltpu.VMEM((NF, PIECE, PIECE, BLK), F32),
            pltpu.SemaphoreType.DMA((TILES // STEP,)),
            pltpu.SemaphoreType.DMA((14,)),
            pltpu.SemaphoreType.DMA((8,)),
            pltpu.SemaphoreType.DMA((8,)),
        ],
        compiler_params=pltpu.CompilerParams(
            collective_id=0, has_side_effects=True, vmem_limit_bytes=60 << 20
        ),
    )(
        features,
        self_weight,
        neighbor_weight,
        unit_bias,
        jnp.transpose(send_blocks, (0, 2, 1)),
        send_counts,
        tile_target,
        tile_source,
        tile_count.reshape(1, 1),
        tile_weights,
        out_grad,
    )
    hidden, selfg, neighg, biasg = pl.pallas_call(
        hand_over,
        out_shape=shapes,
        in_specs=[vmem] * 4,
        out_specs=(vmem,) * 4,
    )(*[pltpu.with_memory_space_constraint(one, pltpu.VMEM) for one in made])
    return hidden, selfg, neighg, biasg.reshape(HU)


def solution(mesh):
    in_specs = (
        P("feat", "dom"),
        P("feat", None),
        P("feat", None),
        P("feat"),
        P("dom", None, None),
        P("dom", None),
        P("dom", None),
        P("dom", None),
        P("dom"),
        P("dom", None, None, None),
        P("feat", "dom"),
    )
    out_specs = (P("feat", "dom"), P("feat", None), P("feat", None), P("feat"))
    return jax.shard_map(body, mesh=mesh, in_specs=in_specs, out_specs=out_specs, check_vma=False)
```
